256 devices in a mesh: seq: 32 (over y, x, core), tp: 8 (over z).
Axes of the slice: x: 4, y: 4, z: 8, core: 2. Of those that a mesh axis runs over, the one named last changes fastest.
Arguments:
- queries: bfloat16 [32, 64, 4096], P('seq', None, 'tp'), may hold values from -8 to 8
- draft_kv: bfloat16 [32, 64, 8, 128], P('seq', None, 'tp'), may hold values from -12.5 to 12.5
- cache_kv: bfloat16 [8, 16384, 8, 128], P(None, 'seq', 'tp'), may hold values from -10 to 10
- cache_len: int32 [8], replicated, may hold values from 4096 to 16384
- group_of: int32 [32], replicated, may hold values from 0 to 7, as said below
- parents: int32 [32, 64], P('seq'), may hold values from 0 to 62, as said below
- sink_logit: float32 [64], P('tp'), may hold values from 4 to 20
- w_out: bfloat16 [4096, 2880], P('tp'), may hold values from -0.09375 to 0.09375
- hidden_in: bfloat16 [2048, 2880], P('seq', 'tp'), may hold values from -3 to 3
- norm_gain: float32 [2880], replicated, may hold values from 0.5 to 1.5
- routes: int32 [2048, 4], P('seq'), may hold values from 0 to 31, all different within a row; in each aligned block of 64 rows (0 to 63, 64 to 127, ...) at most 16 rows name the same one
- route_weight: float32 [2048, 4], P('seq'), may hold values from 0.1 to 1
- w_gate_up: bfloat16 [32, 2, 2880, 2880], P('seq', None, None, 'tp'), may hold values from -0.109375 to 0.109375
- w_down: bfloat16 [32, 2880, 2880], P('seq', 'tp'), may hold values from -0.109375 to 0.109375
- accepted_idx: int32 [32, 16], P('seq'), may hold values from 0 to 45, as said below
- accepted_len: int32 [32], P('seq'), may hold values from 1 to 16, as said below
- tail_slot: int32 [32], replicated, may hold values from 0 to 31, each once
Outputs:
- out_hidden: bfloat16 [2048, 2880], P('seq', 'tp')
- new_tail: bfloat16 [32, 16, 8, 128], P('seq', None, 'tp')
The draws below stay inside these ranges and needn't reach their ends.
Inputs may be any that keep to these rules, and one draw needn't show every extreme that they name: `parents`: node 0 of every tree is its root and its own parent; every other node's parent is one of the three nodes before it. `accepted_idx`: row r lists the first 16 nodes of a path from the root of request r's tree down to one of its last four nodes, root first. `accepted_len`: each request accepts one or more nodes. `group_of`: every prompt group has exactly 4 requests. `routes`: the 4 experts of a token differ; at most 16 of one device's rows (one aligned block of 64 tokens) name one expert.
All inputs are finite; a program needn't handle non-finite values.
Results may differ from the reference program's by a relative error of at most 0.025.
Values may be sent and summed in bfloat16 or wider, within the bound.
A program may use at most 128 MiB of HBM per device.

```python
import math
import jax
import jax.numpy as jnp
import numpy as np
from jax import lax

D = 2880
FF = 2880
HQ = 64
KVH = 8
HD = 64
TOPK = 4
TREE = 64
BLK = 16
CACHE = 16384
RPG = 4
REQUESTS = 32
TOK_DEV = 64
TOKENS = 2048
GROUPS = 8
EXPERTS = 32
CAP = 16
N_SEQ = 32
N_TP = 8


def request_dirs(key):
    flips = jax.random.bernoulli(jax.random.fold_in(key, 101), 0.5, (REQUESTS, KVH, HD))
    return jnp.where(flips, 1.0, -1.0).astype(jnp.float32)


def shard_dirs(key):
    flips = jax.random.bernoulli(jax.random.fold_in(key, 212), 0.5, (GROUPS, N_SEQ, KVH, HD))
    signs = jnp.where(flips, 1.0, -1.0).astype(jnp.float32)
    return jnp.repeat(signs, CACHE // N_SEQ, axis=1)


def tree_layout(key):
    tree_key = jax.random.fold_in(key, 404)
    node_ids = jnp.arange(TREE, dtype=jnp.int32)
    row_ids = jnp.arange(REQUESTS, dtype=jnp.int32)
    deep_row = jax.random.randint(jax.random.fold_in(tree_key, 2), (), 0, REQUESTS)
    steps_back = jax.random.randint(tree_key, (REQUESTS, TREE), 1, 4)
    steps_back = jnp.where((row_ids == deep_row)[:, None], 3, steps_back)
    parents = jnp.maximum(node_ids[None, :] - steps_back, 0).astype(jnp.int32)
    linked = ((parents[:, :, None] == node_ids[None, None, :]) | (node_ids[:, None] == node_ids[None, :])[None]).astype(jnp.int32)
    reachable = linked
    for repeat in range((TREE - 1).bit_length()):
        reachable = jnp.minimum(jnp.matmul(reachable, reachable), 1)
    end_node = TREE - 1 - jax.random.randint(jax.random.fold_in(tree_key, 1), (REQUESTS,), 0, 4)
    end_node = jnp.where(row_ids == deep_row, TREE - 1 - (TREE - 1) % 3, end_node)
    on_path = reachable[row_ids, end_node]
    counted = jnp.cumsum(on_path, axis=1)
    depth_ids = jnp.arange(BLK, dtype=jnp.int32) + 1
    path = jnp.sum(node_ids[None, None, :] * on_path[:, None, :] * (counted[:, None, :] == depth_ids[None, :, None]).astype(jnp.int32), axis=2)
    return (parents, path.astype(jnp.int32))


def draw_parents(key, part):
    return tree_layout(key)[0]


def draw_accepted_idx(key, part):
    return tree_layout(key)[1]


def draw_accepted_len(key, part):
    lengths = jax.random.randint(jax.random.fold_in(key, 808), (REQUESTS,), 1, BLK + 1)
    forced = jax.random.randint(jax.random.fold_in(key, 809), (), 0, REQUESTS)
    row_ids = jnp.arange(REQUESTS)
    lengths = jnp.where(row_ids == (forced + 1) % REQUESTS, 1, lengths)
    return jnp.where(row_ids == forced, BLK, lengths).astype(jnp.int32)


def draw_group_of(key, part):
    return (jax.random.permutation(jax.random.fold_in(key, 606), REQUESTS) // RPG).astype(jnp.int32)


def draw_cache_len(key, part):
    lengths = jax.random.randint(jax.random.fold_in(key, 707), (GROUPS,), CACHE // 4, CACHE + 1)
    forced = jax.random.randint(jax.random.fold_in(key, 708), (), 0, GROUPS)
    group_ids = jnp.arange(GROUPS)
    lengths = jnp.where(group_ids == (forced + 1) % GROUPS, CACHE // 4, lengths)
    return jnp.where(group_ids == forced, CACHE, lengths).astype(jnp.int32)


def draw_queries(key, part):
    shape = (REQUESTS, TREE, KVH, HQ // KVH, HD)
    noise_key = jax.random.fold_in(key, 303)
    noise = jax.random.truncated_normal(noise_key, -4.0, 4.0, shape, jnp.float32)
    values = noise + 0.5 * request_dirs(key)[:, None, :, None, :]
    return values.reshape(REQUESTS, TREE, HQ * HD).astype(jnp.bfloat16)


def draw_draft_kv(key, part):
    shape = (REQUESTS, TREE, KVH, HD)
    first_key = jax.random.fold_in(key, 505)
    second_key = jax.random.fold_in(key, 506)
    key_noise = jax.random.truncated_normal(first_key, -4.0, 4.0, shape, jnp.float32)
    value_noise = jax.random.truncated_normal(second_key, -4.0, 4.0, shape, jnp.float32)
    key_part = 2.5 * key_noise + 2.5 * request_dirs(key)[:, None, :, :]
    return jnp.concatenate([key_part, value_noise], axis=-1).astype(jnp.bfloat16)


def draw_cache_kv(key, part):
    shape = (GROUPS, CACHE, KVH, HD)
    first_key = jax.random.fold_in(key, 515)
    second_key = jax.random.fold_in(key, 516)
    offsets_part = 4.0 * shard_dirs(key)
    key_part = 2.5 * jax.random.truncated_normal(first_key, -4.0, 4.0, shape, jnp.float32)
    value_part = jax.random.truncated_normal(second_key, -4.0, 4.0, shape, jnp.float32) + offsets_part
    return jnp.concatenate([key_part, value_part], axis=-1).astype(jnp.bfloat16)


def block_levels(own_key, dims, cuts, least, high):
    def one(dim, shards_of):
        heights = jax.random.uniform(jax.random.fold_in(jax.random.fold_in(own_key, 6), dim), (shards_of,), jnp.float32, least / len(cuts), high / len(cuts))
        return jnp.repeat(jnp.exp(heights), dims[dim] // shards_of).reshape((-1,) + (1,) * (len(dims) - dim - 1))

    factor_of = one(*cuts[0])
    for cut in cuts[1:]:
        factor_of = factor_of * one(*cut)
    return factor_of


def deal_out(stream_key, own, number, rows, amount, top, bound, slope):
    ranking = jax.random.permutation(stream_key, amount)
    heavy_load, usual = load_shares(amount, rows * top, bound, slope, True), load_shares(amount, rows * top, bound, slope, False)
    places = jnp.arange(amount)

    def named(tallies, offset_by):
        used = int((tallies > 0).sum())
        fixed = max(1, used // 4)
        shifted = fixed + (places - fixed + offset_by * (used - fixed)) % max(1, amount - fixed)
        return jnp.zeros((amount,), jnp.int32).at[ranking[jnp.where(places < fixed, places, shifted)]].set(jnp.asarray(tallies, jnp.int32))

    tallies = jnp.where(number % 4 == 0, named(heavy_load, number // 4), named(usual, number - number // 4 - 1))
    mixed = jax.random.permutation(jax.random.fold_in(own, 3), amount)
    giver, receiver = mixed[0:amount // 2 * 2:2], mixed[1:amount // 2 * 2:2]
    room = jnp.minimum(tallies[giver] - 1, bound - tallies[receiver]) // 2
    room = jnp.where((giver == ranking[0]) | (receiver == ranking[0]) | (tallies[receiver] == 0), 0, jnp.maximum(room, 0))
    shifted = jax.random.randint(jax.random.fold_in(own, 4), (amount // 2,), 0, 1 << 20) % (room + 1)
    tallies = tallies.at[giver].add(-shifted).at[receiver].add(shifted)
    members = jnp.searchsorted(jnp.cumsum(tallies), jnp.arange(rows * top), side="right").astype(jnp.int32)
    listing = members.reshape(top, rows).T
    listing = listing[jax.random.permutation(jax.random.fold_in(own, 1), rows)]
    offset_by = jax.random.randint(jax.random.fold_in(own, 2), (rows, 1), 0, top)
    return jnp.take_along_axis(listing, (jnp.arange(top)[None, :] + offset_by) % top, axis=1)


def load_shares(number_of, total, most, skew, full):
    portions = [(1 << 20) // math.isqrt(standing ** skew) + 1 for standing in range(1, number_of + 1)]
    largest = most if full else min(most, max(-(-total // number_of), total * portions[0] // sum(portions)))
    least = 1 if total - largest >= number_of - 1 else 0
    given, rest = [largest] + [least] * (number_of - 1), total - largest - least * (number_of - 1)
    while rest > 0:
        candidates = [i for i in range(1, number_of) if given[i] < largest] or [i for i in range(1, number_of) if given[i] < most]
        pool, left = sum([portions[i] for i in candidates]), rest
        for i in candidates:
            more = min(most - given[i], max(1, left * portions[i] // pool), rest)
            given[i] = given[i] + more
            rest = rest - more
    return np.array(given)


def gaussian(own_key, extent, spread, most, cuts=(), kind=jnp.bfloat16):
    result = spread * jax.random.normal(own_key, extent, jnp.float32)
    if cuts:
        result = result * block_levels(own_key, extent, cuts, -0.22, 0.18)
    return jnp.clip(result, -most, most).astype(kind)


def setup_inputs(seed: int = 0) -> dict:
    keys = jax.random.split(jax.random.key(seed), 18)
    queries = draw_queries(jax.random.fold_in(keys[17], 71), 0)
    draft_kv = draw_draft_kv(jax.random.fold_in(keys[17], 71), 0)
    cache_kv = draw_cache_kv(jax.random.fold_in(keys[17], 71), 0)
    cache_len = draw_cache_len(jax.random.fold_in(keys[17], 71), 0)
    group_of = draw_group_of(jax.random.fold_in(keys[17], 71), 0)
    parents = draw_parents(jax.random.fold_in(keys[17], 71), 0)
    sink_logit = jnp.clip(4.0 + 16.0 * jax.random.uniform(keys[6], (HQ,), jnp.float32) ** block_levels(keys[6], (HQ,), ((0, 8),), -0.2, 0.2), 4.0, 20.0)
    w_out = gaussian(keys[7], (HQ * HD, D), (HQ * HD) ** -0.5, 0.09375, ((0, 8),))
    hidden_in = gaussian(keys[8], (TOKENS, D), 0.5, 3.0, ((0, 32), (1, 8)))
    norm_gain = jnp.clip(1.0 + 0.1 * jax.random.normal(keys[9], (D,), jnp.float32), 0.5, 1.5)
    routes_keys = jax.random.split(jax.random.fold_in(keys[10], 1), TOKENS // TOK_DEV)
    routes_turns = jax.random.permutation(jax.random.fold_in(keys[10], 3), TOKENS // TOK_DEV)
    routes = jax.vmap(lambda own, number: deal_out(jax.random.fold_in(keys[10], 2), own, number, TOK_DEV, EXPERTS, TOPK, CAP, 2))(routes_keys, routes_turns).reshape((TOKENS, TOPK))
    route_weight = jnp.clip(jnp.exp(math.log(1.0) - 2.3025851 * jax.random.uniform(keys[11], (TOKENS, TOPK), jnp.float32) ** block_levels(keys[11], (TOKENS, TOPK), ((0, 32),), -0.2, 0.2)), 0.1, 1.0)
    w_gate_up = gaussian(keys[12], (EXPERTS, 2, D, FF), D ** -0.5, 0.109375, ((0, 32), (3, 8)))
    w_down = gaussian(keys[13], (EXPERTS, FF, D), FF ** -0.5, 0.109375, ((0, 32), (1, 8)))
    accepted_idx = draw_accepted_idx(jax.random.fold_in(keys[17], 71), 0)
    accepted_len = draw_accepted_len(jax.random.fold_in(keys[17], 71), 0)
    tail_slot = jax.random.permutation(keys[16], REQUESTS).astype(jnp.int32)
    return dict(queries=queries, draft_kv=draft_kv, cache_kv=cache_kv, cache_len=cache_len, group_of=group_of, parents=parents, sink_logit=sink_logit, w_out=w_out, hidden_in=hidden_in, norm_gain=norm_gain, routes=routes, route_weight=route_weight, w_gate_up=w_gate_up, w_down=w_down, accepted_idx=accepted_idx, accepted_len=accepted_len, tail_slot=tail_slot)


def ancestry(parents):
    tree_len = parents.shape[1]
    node_ids = jnp.arange(tree_len, dtype=jnp.int32)
    linked = (parents[:, :, None] == node_ids[None, None, :]) | (node_ids[:, None] == node_ids[None, :])[None]
    reachable = linked.astype(jnp.float32)
    for repeat in range((tree_len - 1).bit_length()):
        reachable = jnp.minimum(jnp.einsum('rij,rjk->rik', reachable, reachable, precision=lax.Precision.HIGHEST), 1.0)
    return reachable

def attend_request(request, queries, draft_kv, cache_kv, cache_len, group_of, reachable, sink_logit):
    per_kv = HQ // KVH
    shard_len = CACHE // N_SEQ
    group_id = group_of[request]
    head_rows = queries[request].astype(jnp.float32).reshape(TREE, KVH, per_kv, HD)
    cached = cache_kv[group_id].astype(jnp.float32).reshape(N_SEQ, shard_len, KVH, 2 * HD)
    positions = jnp.arange(CACHE, dtype=jnp.int32).reshape(N_SEQ, shard_len)
    usable = (positions < cache_len[group_id])[:, None, None, None, :]
    scores = jnp.einsum('tkqd,sckd->skqtc', head_rows, cached[..., :HD], precision=lax.Precision.HIGHEST) * 0.125
    masked = jnp.where(usable, scores, -1e+30)
    shard_max = lax.optimization_barrier(jnp.max(masked, axis=-1))
    weights = jnp.where(usable, jnp.exp(masked - shard_max[..., None]), 0.0)
    shard_sum = lax.optimization_barrier(jnp.sum(weights, axis=-1))
    rounded = lax.optimization_barrier(weights.astype(jnp.bfloat16)).astype(jnp.float32)
    shard_out = jnp.einsum('skqtc,sckd->skqtd', rounded, cached[..., HD:], precision=lax.Precision.HIGHEST)
    shard_out = (shard_out / jnp.maximum(shard_sum, 1.0)[..., None]).astype(jnp.bfloat16)
    draft = draft_kv[request].astype(jnp.float32)
    tree_scores = jnp.einsum('tkqd,ukd->kqtu', head_rows, draft[..., :HD], precision=lax.Precision.HIGHEST) * 0.125
    allowed = (reachable[request] > 0.5)[None, None]
    tree_masked = jnp.where(allowed, tree_scores, -1e+30)
    tree_max = lax.optimization_barrier(jnp.max(tree_masked, axis=-1))
    tree_weight = jnp.where(allowed, jnp.exp(tree_masked - tree_max[..., None]), 0.0)
    tree_sum = lax.optimization_barrier(jnp.sum(tree_weight, axis=-1))
    tree_rounded = lax.optimization_barrier(tree_weight.astype(jnp.bfloat16)).astype(jnp.float32)
    tree_num = jnp.einsum('kqtu,ukd->kqtd', tree_rounded, draft[..., HD:], precision=lax.Precision.HIGHEST)
    sink_rows = sink_logit.reshape(KVH, per_kv)[:, :, None]
    ceiling = jnp.maximum(jnp.maximum(lax.optimization_barrier(jnp.max(shard_max, axis=0)), tree_max), sink_rows)
    shard_scale = shard_sum * jnp.exp(shard_max - ceiling[None])
    tree_scale = jnp.exp(tree_max - ceiling)
    denominator = lax.optimization_barrier(jnp.sum(shard_scale, axis=0)) + tree_scale * tree_sum + jnp.exp(sink_rows - ceiling)
    numerator = lax.optimization_barrier(jnp.sum(shard_scale[..., None] * shard_out.astype(jnp.float32), axis=0)) + tree_scale[..., None] * tree_num
    attention = numerator / denominator[..., None]
    return attention.transpose(2, 0, 1, 3).reshape(TREE, HQ * HD).astype(jnp.bfloat16)

def expert_apply(picked_rows, gate_up, down_proj):
    gate_proj = jnp.dot(picked_rows, gate_up[0], preferred_element_type=jnp.float32)
    upward = jnp.dot(picked_rows, gate_up[1], preferred_element_type=jnp.float32)
    active = (gate_proj * jax.nn.sigmoid(1.702 * gate_proj) * (upward + 1.0)).astype(jnp.bfloat16)
    slice_len = FF // N_TP
    running = jnp.zeros((picked_rows.shape[0], D), jnp.float32)
    for part_index in range(N_TP):
        part_sum = jnp.dot(active[:, part_index * slice_len:(part_index + 1) * slice_len], down_proj[part_index * slice_len:(part_index + 1) * slice_len], preferred_element_type=jnp.float32)
        running = running + lax.optimization_barrier(part_sum.astype(jnp.bfloat16)).astype(jnp.float32)
    return running.astype(jnp.bfloat16)

def reference(queries, draft_kv, cache_kv, cache_len, group_of, parents, sink_logit, w_out, hidden_in, norm_gain, routes, route_weight, w_gate_up, w_down, accepted_idx, accepted_len, tail_slot):
    reachable = ancestry(parents)
    attention = lax.map(lambda request: attend_request(request, queries, draft_kv, cache_kv, cache_len, group_of, reachable, sink_logit), jnp.arange(REQUESTS, dtype=jnp.int32))
    attention = attention.reshape(TOKENS, HQ * HD)
    projected = jnp.dot(attention, w_out, preferred_element_type=jnp.float32)
    stream = (hidden_in.astype(jnp.float32) + projected).astype(jnp.bfloat16)
    stream_f = stream.astype(jnp.float32)
    inv_scale = lax.rsqrt(lax.optimization_barrier(jnp.mean(stream_f * stream_f, axis=-1, keepdims=True)) + 1e-05)
    normed = (stream_f * inv_scale * norm_gain[None, :]).astype(jnp.bfloat16)
    flat_routes = routes.reshape(N_SEQ, TOK_DEV * TOPK)
    onehot = (flat_routes[..., None] == jnp.arange(EXPERTS, dtype=jnp.int32)[None, None, :]).astype(jnp.int32)
    before = jnp.cumsum(onehot, axis=1) - onehot
    position = lax.optimization_barrier(jnp.sum(before * onehot, axis=2))
    source = jnp.arange(N_SEQ, dtype=jnp.int32)[:, None]
    bucket = (source * CAP + position).reshape(-1).astype(jnp.int32)
    expert_ids = flat_routes.reshape(-1).astype(jnp.int32)
    token_ids = (jnp.arange(TOKENS * TOPK, dtype=jnp.int32) // TOPK).astype(jnp.int32)
    buffer = jnp.zeros((EXPERTS, N_SEQ * CAP, D), jnp.bfloat16).at[expert_ids, bucket].set(normed[token_ids])
    expert_out = lax.map(lambda packed: expert_apply(packed[0], packed[1], packed[2]), (buffer, w_gate_up, w_down))
    returned = expert_out[expert_ids, bucket].reshape(TOKENS, TOPK, D)
    mixture = lax.optimization_barrier(jnp.sum(route_weight[:, :, None] * returned.astype(jnp.float32), axis=1))
    out_hidden = (stream.astype(jnp.float32) + mixture).astype(jnp.bfloat16)
    chosen = draft_kv[jnp.arange(REQUESTS, dtype=jnp.int32)[:, None], accepted_idx]
    kept_rows = jnp.arange(BLK, dtype=jnp.int32)[None, :] < accepted_len[:, None]
    picked_rows = jnp.where(kept_rows[:, :, None, None], chosen, jnp.zeros_like(chosen))
    new_tail = jnp.zeros_like(picked_rows).at[tail_slot].set(picked_rows)
    return (out_hidden, new_tail)
```

```python
import jax
import jax.numpy as jnp
from jax import lax
from jax.experimental import pallas as pl
from jax.experimental.pallas import tpu as pltpu
from jax.sharding import PartitionSpec as P

HQ = 64
KVH = 8
HD = 64
LOW = -1e30
FLOOR = -1e29
MESH = pl.DeviceIdType.MESH
BF = jnp.bfloat16
F32 = jnp.float32


def dot(a, b):
    return jnp.dot(a, b, preferred_element_type=F32)


def dot_tn(a, b):
    return lax.dot_general(a, b, (((0,), (0,)), ((), ())), preferred_element_type=F32)


def place():
    me = lax.axis_index("seq")
    core = me % 2
    chip = me // 2
    return me, core, chip // 4, chip % 4, lax.axis_index("tp")


def shifted(y, x, core, d, sign):
    ny = (y + sign * (d // 4) + 4) % 4
    nx = (x + sign * (d % 4) + 4) % 4
    return (ny * 4 + nx) * 2 + core


def remote(src, dst, send, recv, **where):
    return pltpu.make_async_remote_copy(
        src_ref=src, dst_ref=dst, send_sem=send, recv_sem=recv, device_id=where, device_id_type=MESH
    )


def greet(seq_count, tp_count):
    me, tp = lax.axis_index("seq"), lax.axis_index("tp")
    barrier = pltpu.get_barrier_semaphore()

    def over_seq(d, carry):
        pl.semaphore_signal(
            barrier, inc=1, device_id={"seq": (me + d) % seq_count}, device_id_type=MESH
        )
        return carry

    def over_tp(d, carry):
        pl.semaphore_signal(
            barrier, inc=1, device_id={"tp": (tp + d) % tp_count}, device_id_type=MESH
        )
        return carry

    lax.fori_loop(1, seq_count, over_seq, 0)
    lax.fori_loop(1, tp_count, over_tp, 0)
    pl.semaphore_wait(barrier, seq_count + tp_count - 2)


def attention_kernel(
    group_ref, len_ref, sink_ref, slot_ref, alen_ref,
    query_ref, draft_ref, cache_ref, parents_ref, aidx_ref, wout_ref, hidden_ref, gain_ref,
    normed_ref, stream_ref, tail_ref,
    kv, qin, obuf, sbuf, oin, sin, tbuf, tin, att, wout, proj, zsend, zrecv, gsend, gall, full,
    kv_sem, q_send, q_recv, o_send, o_recv, s_send, s_recv, t_sem, w_sem, z_send, z_recv, g_send, g_recv,
):
    me, core, y, x, tp = place()
    chip = y * 4 + x
    greet(32, 8)

    def send_query(d, carry):
        remote(query_ref, qin.at[d], q_send.at[d], q_recv.at[d], seq=shifted(y, x, core, d, 1)).start()
        return carry

    own_half = pltpu.make_async_copy(cache_ref, kv.at[:, core], kv_sem.at[0])
    own_half.start()
    swap = remote(cache_ref, kv.at[:, core], kv_sem.at[1], kv_sem.at[2], seq=chip * 2 + 1 - core)
    swap.start()
    lax.fori_loop(1, 16, send_query, 0)
    load_w = pltpu.make_async_copy(wout_ref, wout, w_sem)
    load_w.start()

    node = lax.broadcasted_iota(jnp.int32, (16, 64), 1)
    row = lax.broadcasted_iota(jnp.int32, (16, 64), 0)
    chosen = jnp.where((node == aidx_ref[...]) & (row < alen_ref[0]), 1.0, 0.0).astype(BF)
    picked = dot(chosen, draft_ref[...]).astype(BF)
    tbuf[...] = picked
    tin[me] = picked

    def send_tail(d, carry):
        remote(tbuf, tin.at[me], t_sem.at[0], t_sem.at[1], seq=(me + d) % 32).start()
        return carry

    lax.fori_loop(1, 32, send_tail, 0)

    query = query_ref[...]
    qin[0] = query
    draft = draft_ref[...]
    zero_q = jnp.zeros((64, 512), BF)
    up_id = lax.broadcasted_iota(jnp.int32, (64, 64), 0)
    node_id = lax.broadcasted_iota(jnp.int32, (64, 64), 1)
    reach = jnp.where((parents_ref[...] == up_id) | (up_id == node_id), 1.0, 0.0)
    for _ in range(6):
        half = reach.astype(BF)
        reach = jnp.minimum(dot(half, half), 1.0)
    allowed = jnp.concatenate([reach] * 8, axis=1) > 0.5
    tree = jnp.where(allowed, dot(draft, jnp.concatenate([query, zero_q], axis=0)), LOW)
    tree_max = jnp.max(tree, axis=0, keepdims=True)
    tree_weight = jnp.where(allowed, jnp.exp(tree - tree_max), 0.0)
    tree_sum = jnp.sum(tree_weight, axis=0, keepdims=True)
    tree_num = dot_tn(draft, tree_weight.astype(BF))[64:]

    own_half.wait()
    swap.wait()
    position = lax.broadcasted_iota(jnp.int32, (1024, 128), 0) + chip * 1024

    def attend(d, carry):
        request = shifted(y, x, core, d, -1)

        @pl.when(d > 0)
        def _():
            remote(query_ref, qin.at[d], q_send.at[d], q_recv.at[d], seq=request).wait_recv()

        group = group_ref[request]
        length = len_ref[group]
        cached = kv[group].reshape(1024, 128)
        bias = jnp.where(position < length, 0.0, LOW)
        bias = jnp.concatenate([bias, bias], axis=1)
        for part in range(2):
            cols = slice(part * 256, part * 256 + 256)
            ask = jnp.concatenate([qin[d, :, cols], jnp.zeros((64, 256), BF)], axis=0)
            score = dot(cached, ask) + bias
            top = jnp.maximum(jnp.max(score, axis=0, keepdims=True), FLOOR)
            weight = jnp.exp(score - top)
            total = jnp.sum(weight, axis=0, keepdims=True)
            value = dot_tn(cached, weight.astype(BF))[64:]
            value = (value / jnp.maximum(total, 1.0)).astype(BF)
            obuf[d, :, cols] = value
            sbuf[d, 0:1, cols] = top
            sbuf[d, 1:2, cols] = total

        @pl.when(d > 0)
        def _():
            remote(obuf.at[d], oin.at[d], o_send.at[d], o_recv.at[d], seq=request).start()
            remote(sbuf.at[d], sin.at[d], s_send.at[d], s_recv.at[d], seq=request).start()

        return carry

    lax.fori_loop(0, 16, attend, 0)
    oin[0] = obuf[0]
    sin[0] = sbuf[0]

    lane = lax.broadcasted_iota(jnp.int32, (1, 512), 1)
    sink = jnp.zeros((1, 512), F32)
    for h in range(8):
        sink = jnp.where(lane // 64 == h, sink_ref[h], sink)

    def land(d, carry):
        other = shifted(y, x, core, d, 1)
        remote(obuf.at[d], oin.at[d], o_send.at[d], o_recv.at[d], seq=other).wait()
        remote(sbuf.at[d], sin.at[d], s_send.at[d], s_recv.at[d], seq=other).wait()
        remote(query_ref, qin.at[d], q_send.at[d], q_recv.at[d], seq=other).wait_send()
        return carry

    lax.fori_loop(1, 16, land, 0)
    ceiling = jnp.maximum(tree_max, sink)
    for d in range(16):
        ceiling = jnp.maximum(ceiling, sin[d, 0:1])
    tree_scale = jnp.exp(tree_max - ceiling)
    below = tree_scale * tree_sum + jnp.exp(sink - ceiling)
    above = tree_scale * tree_num
    for d in range(16):
        scale = sin[d, 1:2] * jnp.exp(sin[d, 0:1] - ceiling)
        below = below + scale
        above = above + scale * oin[d].astype(F32)
    merged = above / below
    for h in range(8):
        att[:, h * 64 : h * 64 + 64] = merged[:, h * 64 : h * 64 + 64].T
    load_w.wait()
    attended = att[...].astype(BF)
    for n in range(0, 2880, 768):
        n_end = min(n + 768, 2880)
        proj[:, n:n_end] = dot(attended, wout[:, n:n_end])

    for j in range(8):
        zsend[j, :, 0:360] = proj[:, 360 * j : 360 * j + 360].astype(BF)

    def send_piece(d, carry):
        to = (tp + d) % 8
        remote(zsend.at[to], zrecv.at[d], z_send.at[d], z_recv.at[d], tp=to).start()
        return carry

    lax.fori_loop(1, 8, send_piece, 0)
    total = hidden_ref[...].astype(F32) + zsend[tp][:, 0:360].astype(F32)
    for d in range(1, 8):
        remote(zsend.at[d], zrecv.at[d], z_send.at[d], z_recv.at[d], tp=(tp + d) % 8).wait()
        total = total + zrecv[d, :, 0:360].astype(F32)
    stream = total.astype(BF)
    stream_ref[...] = stream
    gsend[:, 0:360] = stream
    gall[tp, :, 0:360] = stream

    def send_stream(d, carry):
        to = (tp + d) % 8
        remote(gsend, gall.at[tp], g_send.at[d], g_recv.at[d], tp=to).start()
        return carry

    lax.fori_loop(1, 8, send_stream, 0)

    def land_stream(d, carry):
        remote(gsend, gall.at[(tp - d + 8) % 8], g_send.at[d], g_recv.at[d], tp=(tp + d) % 8).wait()
        return carry

    lax.fori_loop(1, 8, land_stream, 0)
    for j in range(8):
        full[:, 360 * j : 360 * j + 360] = gall[j, :, 0:360].astype(F32)
    rows = full[...]
    scale = lax.rsqrt(jnp.mean(rows * rows, axis=-1, keepdims=True) + 1e-05)
    normed_ref[...] = (rows * scale * gain_ref[...]).astype(BF)

    def drain_tail(ref, sem):
        pltpu.make_async_copy(ref.at[pl.ds(0, 31)], ref.at[pl.ds(0, 31)], sem).wait()

    drain_tail(tin, t_sem.at[0])
    drain_tail(tin, t_sem.at[1])
    kept = jnp.zeros((16, 128), F32)
    for r in range(32):
        kept = kept + jnp.where(slot_ref[r] == me, tin[r].astype(F32), 0.0)
    tail_ref[...] = kept.astype(BF)


def run_attention(group_of, cache_len, sink, tail_slot, accepted_len, query, draft, cache, parents, aidx, w_out, hidden, gain):
    smem = pl.BlockSpec(memory_space=pltpu.SMEM)
    vmem = pl.BlockSpec(memory_space=pltpu.VMEM)
    hbm = pl.BlockSpec(memory_space=pl.ANY)
    dma = pltpu.SemaphoreType.DMA
    return pl.pallas_call(
        attention_kernel,
        out_shape=(
            jax.ShapeDtypeStruct((64, 2880), BF),
            jax.ShapeDtypeStruct((64, 360), BF),
            jax.ShapeDtypeStruct((16, 128), BF),
        ),
        in_specs=[smem] * 5 + [vmem, vmem, hbm, vmem, vmem, hbm, vmem, vmem],
        out_specs=(vmem, vmem, vmem),
        scratch_shapes=[
            pltpu.VMEM((8, 2, 512, 128), BF),
            pltpu.VMEM((16, 64, 512), BF),
            pltpu.VMEM((16, 64, 512), BF),
            pltpu.VMEM((16, 8, 512), F32),
            pltpu.VMEM((16, 64, 512), BF),
            pltpu.VMEM((16, 8, 512), F32),
            pltpu.VMEM((16, 128), BF),
            pltpu.VMEM((32, 16, 128), BF),
            pltpu.VMEM((64, 512), F32),
            pltpu.VMEM((512, 2880), BF),
            pltpu.VMEM((64, 2880), F32),
            pltpu.VMEM((8, 64, 384), BF),
            pltpu.VMEM((8, 64, 384), BF),
            pltpu.VMEM((64, 384), BF),
            pltpu.VMEM((8, 64, 384), BF),
            pltpu.VMEM((64, 2880), F32),
            dma((3,)), dma((16,)), dma((16,)), dma((16,)), dma((16,)), dma((16,)), dma((16,)),
            dma((2,)), dma, dma((8,)), dma((8,)), dma((8,)), dma((8,)),
        ],
        compiler_params=pltpu.CompilerParams(
            collective_id=0, has_side_effects=True, vmem_limit_bytes=48 * 1024 * 1024
        ),
        name="attend",
    )(group_of, cache_len, sink, tail_slot, accepted_len, query, draft, cache, parents, aidx, w_out, hidden, gain)


CHUNKS = ((0, 768), (768, 1536), (1536, 2304), (2304, 2880))


def expert_kernel(
    routes_ref, weight_ref, normed_ref, stream_ref, wgu_ref, wd_ref,
    out_ref,
    wgu, wd, put, mix, acc_g, acc_u, act, comb, zsend, zrecv,
    d0, d1, d2, d3, r0, r1, r2, r3, b0, b1, b2, b3, g0, g1, g2, g3,
    w_sem, d_send, d_recv, b_send, b_recv, z_send, z_recv,
):
    me, core, y, x, tp = place()
    greet(32, 8)
    sent, arrived, back, got = (d0, d1, d2, d3), (r0, r1, r2, r3), (b0, b1, b2, b3), (g0, g1, g2, g3)
    load_gu = pltpu.make_async_copy(wgu_ref, wgu, w_sem.at[0])
    load_gu.start()
    load_d = pltpu.make_async_copy(wd_ref, wd, w_sem.at[1])
    load_d.start()

    expert_id = lax.broadcasted_iota(jnp.int32, (32, 64), 0)
    member = jnp.zeros((32, 64), F32)
    gain = jnp.zeros((32, 64), F32)
    for k in range(4):
        hit = routes_ref[k : k + 1, :] == expert_id
        member = jnp.where(hit, 1.0, member)
        gain = jnp.where(hit, weight_ref[k : k + 1, :], gain)
    earlier = lax.broadcasted_iota(jnp.int32, (64, 64), 0) < lax.broadcasted_iota(jnp.int32, (64, 64), 1)
    rank = dot(member.astype(BF), jnp.where(earlier, 1.0, 0.0).astype(BF))
    slot = lax.broadcasted_iota(jnp.int32, (16, 64), 0).astype(F32)
    for e in range(32):
        here = (slot == rank[e : e + 1, :]) & (member[e : e + 1, :] > 0.5)
        put[e * 16 : e * 16 + 16, :] = jnp.where(here, 1.0, 0.0).astype(BF)
        mix[e * 16 : e * 16 + 16, :] = jnp.where(here, gain[e : e + 1, :], 0.0)

    def spread(src, dst, send, recv):
        def one(d, carry):
            to = (me + d) % 32
            remote(src.at[to], dst.at[me], send, recv, seq=to).start()
            return carry

        lax.fori_loop(1, 32, one, 0)

    def drain(ref, sem):
        pltpu.make_async_copy(ref.at[pl.ds(0, 31)], ref.at[pl.ds(0, 31)], sem).wait()

    for c, (lo, hi) in enumerate(CHUNKS):
        @pl.loop(0, 4)
        def _(b, c=c, lo=lo, hi=hi):
            rows = put[pl.ds(pl.multiple_of(b * 128, 128), 128), :]
            moved = dot(rows, normed_ref[:, lo:hi]).astype(BF)
            sent[c][pl.ds(b * 8, 8)] = moved.reshape(8, 16, hi - lo)

        spread(sent[c], arrived[c], d_send.at[c], d_recv.at[c])
        arrived[c][me] = sent[c][me]

    weight = mix[...].T
    high = weight.astype(BF)
    low = (weight - high.astype(F32)).astype(BF)
    mixing = jnp.concatenate([high, low], axis=0)

    load_gu.wait()
    for c, (lo, hi) in enumerate(CHUNKS):
        drain(arrived[c], d_recv.at[c])

        @pl.loop(0, 2)
        def _(b, c=c, lo=lo, hi=hi):
            rows = arrived[c][pl.ds(b * 16, 16)].reshape(256, hi - lo)
            span = pl.ds(pl.multiple_of(b * 256, 256), 256)
            gate, up = dot(rows, wgu[0, lo:hi, :]), dot(rows, wgu[1, lo:hi, :])
            if c > 0:
                gate, up = gate + acc_g[span, :], up + acc_u[span, :]
            if c < 3:
                acc_g[span, :] = gate
                acc_u[span, :] = up
            else:
                act[span, :] = (gate * jax.nn.sigmoid(1.702 * gate) * (up + 1.0)).astype(BF)

    load_d.wait()
    for c, (lo, hi) in enumerate(CHUNKS):
        @pl.loop(0, 2)
        def _(b, c=c, lo=lo, hi=hi):
            rows = act[pl.ds(pl.multiple_of(b * 256, 256), 256), :]
            down = dot(rows, wd[:, lo:hi]).astype(BF)
            back[c][pl.ds(b * 16, 16)] = down.reshape(16, 16, hi - lo)

        spread(back[c], got[c], b_send.at[c], b_recv.at[c])
        got[c][me] = back[c][me]

    for c, (lo, hi) in enumerate(CHUNKS):
        drain(got[c], b_recv.at[c])
        both = dot(mixing, got[c][...].reshape(512, hi - lo))
        comb[:, lo:hi] = both[0:64] + both[64:128]
        for j in (2 * c, 2 * c + 1):
            zsend[j, :, 0:360] = comb[:, 360 * j : 360 * j + 360].astype(BF)

    def send_piece(d, carry):
        to = (tp + d) % 8
        remote(zsend.at[to], zrecv.at[d], z_send.at[d], z_recv.at[d], tp=to).start()
        return carry

    lax.fori_loop(1, 8, send_piece, 0)
    total = stream_ref[...].astype(F32) + zsend[tp][:, 0:360].astype(F32)
    for d in range(1, 8):
        remote(zsend.at[d], zrecv.at[d], z_send.at[d], z_recv.at[d], tp=(tp + d) % 8).wait()
        total = total + zrecv[d, :, 0:360].astype(F32)
    out_ref[...] = total.astype(BF)
    for c in range(4):
        drain(sent[c], d_send.at[c])
        drain(back[c], b_send.at[c])


def run_experts(routes, weights, normed, stream, w_gate_up, w_down):
    vmem = pl.BlockSpec(memory_space=pltpu.VMEM)
    hbm = pl.BlockSpec(memory_space=pl.ANY)
    dma = pltpu.SemaphoreType.DMA
    blocks = [pltpu.VMEM((32, 16, hi - lo), BF) for lo, hi in CHUNKS]
    return pl.pallas_call(
        expert_kernel,
        out_shape=jax.ShapeDtypeStruct((64, 360), BF),
        in_specs=[vmem] * 4 + [hbm, hbm],
        out_specs=vmem,
        scratch_shapes=[
            pltpu.VMEM((2, 2880, 360), BF),
            pltpu.VMEM((360, 2880), BF),
            pltpu.VMEM((512, 64), BF),
            pltpu.VMEM((512, 64), F32),
            pltpu.VMEM((512, 360), F32),
            pltpu.VMEM((512, 360), F32),
            pltpu.VMEM((512, 360), BF),
            pltpu.VMEM((64, 2880), F32),
            pltpu.VMEM((8, 64, 384), BF),
            pltpu.VMEM((8, 64, 384), BF),
            *blocks, *blocks, *blocks, *blocks,
            dma((2,)), dma((4,)), dma((4,)), dma((4,)), dma((4,)), dma((8,)), dma((8,)),
        ],
        compiler_params=pltpu.CompilerParams(
            collective_id=1, has_side_effects=True, vmem_limit_bytes=56 * 1024 * 1024
        ),
        name="experts",
    )(routes, weights, normed, stream, w_gate_up, w_down)


def shards(
    queries, draft_kv, cache_kv, cache_len, group_of, parents, sink_logit, w_out, hidden_in,
    norm_gain, routes, route_weight, w_gate_up, w_down, accepted_idx, accepted_len, tail_slot,
):
    query = queries.reshape(64, 8, 64).transpose(2, 1, 0).reshape(64, 512) * BF(0.125)
    normed, stream, tail = run_attention(
        group_of, cache_len, sink_logit, tail_slot, accepted_len,
        query, draft_kv.reshape(64, 128), cache_kv.reshape(8, 512, 128), parents,
        accepted_idx.reshape(16, 1), w_out, hidden_in, norm_gain.reshape(1, 2880),
    )
    out = run_experts(
        routes.T, route_weight.T, normed, stream,
        w_gate_up.reshape(2, 2880, 360), w_down.reshape(360, 2880),
    )
    return (out, tail.reshape(1, 16, 1, 128))


def solution(mesh):
    in_specs = (
        P("seq", None, "tp"),
        P("seq", None, "tp", None),
        P(None, "seq", "tp", None),
        P(),
        P(),
        P("seq", None),
        P("tp"),
        P("tp", None),
        P("seq", "tp"),
        P(),
        P("seq", None),
        P("seq", None),
        P("seq", None, None, "tp"),
        P("seq", "tp", None),
        P("seq", None),
        P("seq"),
        P(),
    )
    out_specs = (P("seq", "tp"), P("seq", None, "tp", None))
    return jax.shard_map(shards, mesh=mesh, in_specs=in_specs, out_specs=out_specs, check_vma=False)
```

```python
import jax
import jax.numpy as jnp
from jax import lax
from jax.experimental import pallas as pl
from jax.experimental.pallas import tpu as pltpu
from jax.sharding import PartitionSpec as P

LOW = -1e30
FLOOR = -1e29
MESH = pl.DeviceIdType.MESH
BF = jnp.bfloat16
F32 = jnp.float32


def dot(a, b):
    return jnp.dot(a, b, preferred_element_type=F32)


def dot_tn(a, b):
    return lax.dot_general(a, b, (((0,), (0,)), ((), ())), preferred_element_type=F32)


def dot_nt(a, b):
    return lax.dot_general(a, b, (((1,), (1,)), ((), ())), preferred_element_type=F32)


def remote(src, dst, send, recv, **where):
    return pltpu.make_async_remote_copy(
        src_ref=src, dst_ref=dst, send_sem=send, recv_sem=recv, device_id=where, device_id_type=MESH
    )


def loop(lo, hi, body):
    def step(i, carry):
        body(i)
        return carry

    lax.fori_loop(lo, hi, step, 0)


def layer_kernel(
    group_ref, len_ref, sink_ref, slot_ref, alen_ref,
    query_ref, draft_ref, cache_ref, parents_ref, aidx_ref, wout_ref, hidden_ref, gain_ref,
    routes_ref, weight_ref, wgu_ref, wd_ref,
    out_ref, tail_ref,
    kv, qraw, qown, qin, obuf, sbuf, oin, sin, tbuf, tin, att, wout,
    hpad, zsend, zrecv, piece, gall, ssend, srecv, nq,
    wgu, wgp, wd, wdp, put, mix, sent, arrived, zout, zin, keep, back, got, comb, fsend, frecv,
    kv_sem, q_send, q_recv, o_send, o_recv, s_send, s_recv, t_sem, w_sem,
    z_send, z_recv, g_send, g_recv, n_send, n_recv,
    d_send, d_recv, f_send, f_recv, p_send, p_recv, b_send, b_recv, e_send, e_recv,
):
    me, tp = lax.axis_index("seq"), lax.axis_index("tp")
    core, chip = me % 2, me // 2
    y, x = chip // 4, chip % 4
    odd = tp % 2
    need = ((tp + 2) // 4) % 2

    def peer(d, sign, flip=1):
        ny = (y + sign * (d // 4) + 4) % 4
        nx = (x + sign * (d % 4) + 4) % 4
        return (ny * 4 + nx) * 2 + (core + flip) % 2

    def same(d, sign):
        return peer(d, sign, 0)

    def away(d, sign):
        return peer(d // 2, sign, d % 2)

    barrier = pltpu.get_barrier_semaphore()

    def hello(d):
        pl.semaphore_signal(barrier, inc=1, device_id={"seq": away(d, 1)}, device_id_type=MESH)

    def hello_tp(d):
        pl.semaphore_signal(barrier, inc=1, device_id={"tp": (tp + d) % 8}, device_id_type=MESH)

    loop(1, 32, hello)
    loop(1, 8, hello_tp)

    own_half = pltpu.make_async_copy(cache_ref, kv.at[:, core], kv_sem.at[0])
    own_half.start()
    loads = [
        pltpu.make_async_copy(src, dst, w_sem.at[i])
        for i, (src, dst) in enumerate(((wout_ref, wout), (wgu_ref, wgu), (wd_ref, wd)))
    ]
    for load in loads:
        load.start()

    asked = query_ref[...].astype(F32) * 0.125
    for h in range(8):
        qraw[:, h * 64 : h * 64 + 64] = asked[:, h * 64 : h * 64 + 64].T
    query = qraw[...].astype(BF)
    qown[...] = query
    qin[0] = query
    node = lax.broadcasted_iota(jnp.int32, (64, 16), 0)
    row = lax.broadcasted_iota(jnp.int32, (64, 16), 1)
    chosen = jnp.where((node == aidx_ref[...]) & (row < alen_ref[0]), 1.0, 0.0).astype(BF)
    picked = dot_tn(chosen, draft_ref[...]).astype(BF)
    tbuf[...] = picked
    tin[me] = picked

    pl.semaphore_wait(barrier, 38)
    swap = remote(cache_ref, kv.at[:, core], kv_sem.at[1], kv_sem.at[2], seq=chip * 2 + 1 - core)
    swap.start()

    def send_query(d):
        remote(qown, qin.at[d], q_send.at[d], q_recv.at[d], seq=same(d, 1)).start()

    loop(1, 16, send_query)

    def send_tail(d):
        remote(tbuf, tin.at[me], t_sem.at[0], t_sem.at[1], seq=away(d, 1)).start()

    loop(1, 32, send_tail)

    draft = draft_ref[...]
    up_id = lax.broadcasted_iota(jnp.int32, (64, 64), 0)
    node_id = lax.broadcasted_iota(jnp.int32, (64, 64), 1)
    reach = jnp.where((parents_ref[...] == up_id) | (up_id == node_id), 1.0, 0.0)
    for _ in range(6):
        half = reach.astype(BF)
        reach = jnp.minimum(dot(half, half), 1.0)
    allowed = jnp.concatenate([reach] * 8, axis=1) > 0.5
    tree = jnp.where(allowed, dot(draft, jnp.concatenate([query, jnp.zeros((64, 512), BF)], axis=0)), LOW)
    tree_max = jnp.max(tree, axis=0, keepdims=True)
    tree_weight = jnp.where(allowed, jnp.exp(tree - tree_max), 0.0)
    tree_sum = jnp.sum(tree_weight, axis=0, keepdims=True)
    tree_num = dot_tn(draft, tree_weight.astype(BF))[64:]

    own_half.wait()
    swap.wait()
    position = lax.broadcasted_iota(jnp.int32, (1024, 128), 0) + chip * 1024

    def attend(d):
        request = same(d, -1)

        @pl.when(d > 0)
        def _():
            remote(qown, qin.at[d], q_send.at[d], q_recv.at[d], seq=request).wait_recv()

        group = group_ref[request]
        length = len_ref[group]
        cached = kv[group].reshape(1024, 128)
        bias = jnp.where(position < length, 0.0, LOW)
        bias = jnp.concatenate([bias, bias], axis=1)
        for part in range(2):
            cols = slice(part * 256, part * 256 + 256)
            ask = jnp.concatenate([qin[d, :, cols], jnp.zeros((64, 256), BF)], axis=0)
            score = dot(cached, ask) + bias
            top = jnp.maximum(jnp.max(score, axis=0, keepdims=True), FLOOR)
            weight = jnp.exp(score - top)
            total = jnp.sum(weight, axis=0, keepdims=True)
            value = dot_tn(cached, weight.astype(BF))[64:]
            obuf[d, :, cols] = (value / jnp.maximum(total, 1.0)).astype(BF)
            sbuf[d, 0:1, cols] = top
            sbuf[d, 1:2, cols] = total

        @pl.when(d > 0)
        def _():
            remote(obuf.at[d], oin.at[d], o_send.at[d], o_recv.at[d], seq=request).start()
            remote(sbuf.at[d], sin.at[d], s_send.at[d], s_recv.at[d], seq=request).start()

    loop(0, 16, attend)
    oin[0] = obuf[0]
    sin[0] = sbuf[0]

    expert_id = lax.broadcasted_iota(jnp.int32, (32, 64), 0)
    member = jnp.zeros((32, 64), F32)
    given = jnp.zeros((32, 64), F32)
    for k in range(4):
        hit = routes_ref[k : k + 1, :] == expert_id
        member = jnp.where(hit, 1.0, member)
        given = jnp.where(hit, weight_ref[k : k + 1, :], given)
    rank = dot(member.astype(BF), jnp.where(up_id < node_id, 1.0, 0.0).astype(BF))
    slot = lax.broadcasted_iota(jnp.int32, (16, 64), 0).astype(F32)
    for e in range(32):
        here = (slot == rank[e : e + 1, :]) & (member[e : e + 1, :] > 0.5)
        put[e * 16 : e * 16 + 16, :] = jnp.where(here, 1.0, 0.0).astype(BF)
        mix[e * 16 : e * 16 + 16, :] = jnp.where(here, given[e : e + 1, :], 0.0)
    for load in loads:
        load.wait()
    blank = jnp.zeros((360, 24), BF)
    for j in range(8):
        span, wide = slice(360 * j, 360 * j + 360), slice(384 * j, 384 * j + 384)
        wgp[0, :, wide] = jnp.concatenate([wgu[0, :, span], blank], axis=1)
        wgp[1, :, wide] = jnp.concatenate([wgu[1, :, span], blank], axis=1)
        wdp[:, wide] = jnp.concatenate([wd[:, span], blank], axis=1)
    zsend[...] = jnp.zeros((8, 64, 384), BF)
    hpad[...] = jnp.zeros((64, 384), F32)
    hpad[:, 0:360] = hidden_ref[...].astype(F32)

    lane = lax.broadcasted_iota(jnp.int32, (1, 512), 1)
    sink = jnp.zeros((1, 512), F32)
    for h in range(8):
        sink = jnp.where(lane // 64 == h, sink_ref[h], sink)

    def land(d):
        other = same(d, 1)
        remote(obuf.at[d], oin.at[d], o_send.at[d], o_recv.at[d], seq=other).wait()
        remote(sbuf.at[d], sin.at[d], s_send.at[d], s_recv.at[d], seq=other).wait()
        remote(qown, qin.at[d], q_send.at[d], q_recv.at[d], seq=other).wait_send()

    loop(1, 16, land)
    ceiling = jnp.maximum(tree_max, sink)
    for d in range(16):
        ceiling = jnp.maximum(ceiling, sin[d, 0:1])
    tree_scale = jnp.exp(tree_max - ceiling)
    below = tree_scale * tree_sum + jnp.exp(sink - ceiling)
    above = tree_scale * tree_num
    for d in range(16):
        scale = sin[d, 1:2] * jnp.exp(sin[d, 0:1] - ceiling)
        below = below + scale
        above = above + scale * oin[d].astype(F32)
    merged = above / below
    for h in range(8):
        att[:, h * 64 : h * 64 + 64] = merged[:, h * 64 : h * 64 + 64].T
    attended = att[...].astype(BF)
    for j in range(8):
        zsend[j, :, 0:360] = dot_nt(attended, wout[360 * j : 360 * j + 360, :]).astype(BF)

    def send_piece(d):
        to = (tp + d) % 8
        remote(zsend.at[to], zrecv.at[d], z_send.at[d], z_recv.at[d], tp=to).start()

    loop(1, 8, send_piece)
    total = hpad[...] + zsend[tp].astype(F32)
    for d in range(1, 8):
        remote(zsend.at[d], zrecv.at[d], z_send.at[d], z_recv.at[d], tp=(tp + d) % 8).wait()
        total = total + zrecv[d].astype(F32)
    stream = total.astype(BF)
    piece[...] = stream
    stream_f = stream.astype(F32)

    for k in range(4):
        to = 2 * k + need

        @pl.when(to != tp)
        def _(k=k, to=to):
            remote(piece, gall.at[tp % 4], g_send.at[k], g_recv.at[tp % 4], tp=to).start()

        @pl.when(to == tp)
        def _():
            gall[tp % 4] = piece[...]

    squares = jnp.sum(stream_f * stream_f, axis=1, keepdims=True)
    square = jnp.broadcast_to(squares, (64, 128))
    spread_rows = jnp.concatenate([square, square], axis=0).T[0:8]
    ssend[...] = spread_rows

    def send_norm(d):
        remote(ssend, srecv.at[d], n_send.at[d], n_recv.at[d], tp=(tp + d) % 8).start()

    loop(1, 8, send_norm)
    summed = spread_rows
    for d in range(1, 8):
        remote(ssend, srecv.at[d], n_send.at[d], n_recv.at[d], tp=(tp + d) % 8).wait()
        summed = summed + srecv[d]
    column = jnp.concatenate([summed] * 16, axis=0).T[0:64, 0:1]
    inverse = lax.rsqrt(column * (1.0 / 2880.0) + 1e-05)

    for k in range(4):
        source = k + 4 * ((k // 2 + odd) % 2)

        @pl.when(source != tp)
        def _(k=k, source=source):
            remote(piece, gall.at[k], g_send.at[k], g_recv.at[k], tp=source).wait_recv()

    mine = (odd, 3 - odd)
    for h in range(2):
        for i in range(2):
            j = 2 * mine[h] + i
            normed = gall[j % 4].astype(F32) * inverse * gain_ref[j]
            nq[h, :, 384 * i : 384 * i + 384] = normed.astype(BF)

    for h in range(2):
        @pl.loop(0, 4)
        def _(b, h=h):
            rows = put[pl.ds(pl.multiple_of(b * 128, 128), 128), :]
            sent[h, pl.ds(b * 8, 8)] = dot(rows, nq[h]).astype(BF).reshape(8, 16, 768)

    def dispatch(d):
        to = away(d, 1)
        for h in range(2):
            remote(sent.at[h, to], arrived.at[mine[h], d], d_send.at[h], d_recv.at[h, d], seq=to).start()

    loop(1, 32, dispatch)
    for h in range(2):
        arrived[mine[h], 0] = sent[h, me]

    partner = (tp + 1 - 2 * odd, (tp + 7 + 2 * odd) % 8)
    other = (1 - odd, 2 + odd)

    def forward(d):
        for h in range(2):
            @pl.when(d > 0)
            def _(h=h):
                remote(
                    sent.at[h, 0], arrived.at[mine[h], d], d_send.at[h], d_recv.at[h, d], seq=away(d, -1)
                ).wait_recv()

            block = arrived.at[mine[h], d]
            remote(block, block, f_send.at[h], f_recv.at[h, d // 8], tp=partner[h]).start()

    def feed(g):
        for h in range(2):
            block = arrived.at[other[h], pl.ds(g * 8, 8)]
            pltpu.make_async_copy(block, block, f_recv.at[h, g]).wait()
        gate = jnp.zeros((128, 360), F32)
        up = jnp.zeros((128, 360), F32)
        for q in range(4):
            rows = arrived[q, pl.ds(g * 8, 8)].reshape(128, 768)
            cols = slice(768 * q, 768 * q + 768)
            gate = gate + dot_nt(rows, wgp[0, :, cols])
            up = up + dot_nt(rows, wgp[1, :, cols])
        act = (gate * jax.nn.sigmoid(1.702 * gate) * (up + 1.0)).astype(BF)
        for h in range(2):
            far = dot(act, wdp[:, pl.ds(pl.multiple_of(768 * other[h], 128), 768)])
            zout[h, g] = far.astype(BF).reshape(8, 16, 768)
            remote(zout.at[h, g], zin.at[h, g], p_send.at[h, g], p_recv.at[h, g], tp=partner[h]).start()
        for h in range(2):
            keep[h, g] = dot(act, wdp[:, pl.ds(pl.multiple_of(768 * mine[h], 128), 768)])

    def give(g):
        for h in range(2):
            remote(zout.at[h, g], zin.at[h, g], p_send.at[h, g], p_recv.at[h, g], tp=partner[h]).wait()
            both = keep[h, g] + zin[h, g].reshape(128, 768).astype(F32)
            back[h, pl.ds(g * 8, 8)] = both.astype(BF).reshape(8, 16, 768)

        def one(i):
            d = g * 8 + i
            for h in range(2):
                @pl.when(d > 0)
                def _(h=h):
                    to = away(d, -1)
                    remote(back.at[h, d], got.at[h, me], b_send.at[h], b_recv.at[h], seq=to).start()

        loop(0, 8, one)

    def stage(i):
        @pl.when(i < 4)
        def _():
            loop(i * 8, i * 8 + 8, forward)

        @pl.when((i > 0) & (i < 5))
        def _():
            feed(i - 1)

        @pl.when(i > 1)
        def _():
            give(i - 2)

    loop(0, 6, stage)
    for h in range(2):
        got[h, me] = back[h, 0]

    weight = mix[...].T
    high = weight.astype(BF)
    low = (weight - high.astype(F32)).astype(BF)
    mixing = jnp.concatenate([high, low], axis=0)

    def drain(ref, sem):
        pltpu.make_async_copy(ref.at[pl.ds(0, 31)], ref.at[pl.ds(0, 31)], sem).wait()

    for h in range(2):
        drain(got.at[h], b_recv.at[h])
        both = dot(mixing, got[h].reshape(512, 768))
        both = both[0:64] + both[64:128]
        for i in range(2):
            k = 2 * h + i
            to = 2 * mine[h] + i
            fsend[k] = both[:, 384 * i : 384 * i + 384].astype(BF)

            @pl.when(to != tp)
            def _(k=k, to=to):
                remote(fsend.at[k], frecv.at[tp // 2], e_send.at[k], e_recv.at[tp // 2], tp=to).start()

            @pl.when(to == tp)
            def _(k=k):
                frecv[tp // 2] = fsend[k]

    total = piece[...].astype(F32)
    for k in range(4):
        source = 2 * k + need

        @pl.when(source != tp)
        def _(k=k, source=source):
            remote(fsend.at[k], frecv.at[k], e_send.at[k], e_recv.at[k], tp=source).wait_recv()

        total = total + frecv[k].astype(F32)
    out_ref[...] = total[:, 0:360].astype(BF)

    drain(tin, t_sem.at[0])
    drain(tin, t_sem.at[1])
    kept = jnp.zeros((16, 128), F32)
    for r in range(32):
        kept = kept + jnp.where(slot_ref[r] == me, tin[r].astype(F32), 0.0)
    tail_ref[...] = kept.astype(BF)

    for k in range(4):
        @pl.when(2 * k + need != tp)
        def _(k=k):
            remote(piece, gall.at[k], g_send.at[k], g_recv.at[k], tp=2 * k + need).wait_send()

        to = 2 * mine[k // 2] + k % 2

        @pl.when(to != tp)
        def _(k=k, to=to):
            remote(fsend.at[k], frecv.at[k], e_send.at[k], e_recv.at[k], tp=to).wait_send()

    for h in range(2):
        drain(sent.at[h], d_send.at[h])
        drain(back.at[h], b_send.at[h])
        pltpu.make_async_copy(sent.at[h], sent.at[h], f_send.at[h]).wait()


def run_layer(*operands):
    smem = pl.BlockSpec(memory_space=pltpu.SMEM)
    vmem = pl.BlockSpec(memory_space=pltpu.VMEM)
    hbm = pl.BlockSpec(memory_space=pl.ANY)
    dma = pltpu.SemaphoreType.DMA
    return pl.pallas_call(
        layer_kernel,
        out_shape=(jax.ShapeDtypeStruct((64, 360), BF), jax.ShapeDtypeStruct((16, 128), BF)),
        in_specs=[smem] * 5 + [vmem, vmem, hbm, vmem, vmem, hbm, vmem, vmem, vmem, vmem, hbm, hbm],
        out_specs=(vmem, vmem),
        scratch_shapes=[
            pltpu.VMEM((8, 2, 512, 128), BF),
            pltpu.VMEM((64, 512), F32),
            pltpu.VMEM((64, 512), BF),
            pltpu.VMEM((16, 64, 512), BF),
            pltpu.VMEM((16, 64, 512), BF),
            pltpu.VMEM((16, 2, 512), F32),
            pltpu.VMEM((16, 64, 512), BF),
            pltpu.VMEM((16, 2, 512), F32),
            pltpu.VMEM((16, 128), BF),
            pltpu.VMEM((32, 16, 128), BF),
            pltpu.VMEM((64, 512), F32),
            pltpu.VMEM((2880, 512), BF),
            pltpu.VMEM((64, 384), F32),
            pltpu.VMEM((8, 64, 384), BF),
            pltpu.VMEM((8, 64, 384), BF),
            pltpu.VMEM((64, 384), BF),
            pltpu.VMEM((4, 64, 384), BF),
            pltpu.VMEM((8, 128), F32),
            pltpu.VMEM((8, 8, 128), F32),
            pltpu.VMEM((2, 64, 768), BF),
            pltpu.VMEM((2, 360, 2880), BF),
            pltpu.VMEM((2, 360, 3072), BF),
            pltpu.VMEM((360, 2880), BF),
            pltpu.VMEM((360, 3072), BF),
            pltpu.VMEM((512, 64), BF),
            pltpu.VMEM((512, 64), F32),
            pltpu.VMEM((2, 32, 16, 768), BF),
            pltpu.VMEM((4, 32, 16, 768), BF),
            pltpu.VMEM((2, 4, 8, 16, 768), BF),
            pltpu.VMEM((2, 4, 8, 16, 768), BF),
            pltpu.VMEM((2, 4, 128, 768), F32),
            pltpu.VMEM((2, 32, 16, 768), BF),
            pltpu.VMEM((2, 32, 16, 768), BF),
            pltpu.VMEM((8, 128), F32),
            pltpu.VMEM((4, 64, 384), BF),
            pltpu.VMEM((4, 64, 384), BF),
            dma((3,)), dma((16,)), dma((16,)), dma((16,)), dma((16,)), dma((16,)), dma((16,)),
            dma((2,)), dma((3,)),
            dma((8,)), dma((8,)), dma((4,)), dma((4,)), dma((8,)), dma((8,)),
            dma((2,)), dma((2, 32)), dma((2,)), dma((2, 4)), dma((2, 4)), dma((2, 4)),
            dma((2,)), dma((2,)), dma((4,)), dma((4,)),
        ],
        compiler_params=pltpu.CompilerParams(
            collective_id=0, has_side_effects=True, vmem_limit_bytes=62 * 1024 * 1024
        ),
        name="layer",
    )(*operands)


def shards(
    queries, draft_kv, cache_kv, cache_len, group_of, parents, sink_logit, w_out, hidden_in,
    norm_gain, routes, route_weight, w_gate_up, w_down, accepted_idx, accepted_len, tail_slot,
):
    gain = jnp.pad(norm_gain.reshape(8, 1, 360), ((0, 0), (0, 0), (0, 24)))
    out, tail = run_layer(
        group_of, cache_len, sink_logit, tail_slot, accepted_len,
        queries.reshape(64, 512), draft_kv.reshape(64, 128), cache_kv.reshape(8, 512, 128), parents,
        accepted_idx, w_out.T, hidden_in, gain, routes.T, route_weight.T,
        w_gate_up.reshape(2, 2880, 360).transpose(0, 2, 1), w_down.reshape(360, 2880),
    )
    return (out, tail.reshape(1, 16, 1, 128))


def solution(mesh):
    in_specs = (
        P("seq", None, "tp"),
        P("seq", None, "tp", None),
        P(None, "seq", "tp", None),
        P(),
        P(),
        P("seq", None),
        P("tp"),
        P("tp", None),
        P("seq", "tp"),
        P(),
        P("seq", None),
        P("seq", None),
        P("seq", None, None, "tp"),
        P("seq", "tp", None),
        P("seq", None),
        P("seq"),
        P(),
    )
    out_specs = (P("seq", "tp"), P("seq", None, "tp", None))
    return jax.shard_map(shards, mesh=mesh, in_specs=in_specs, out_specs=out_specs, check_vma=False)
```

```python
import jax
import jax.numpy as jnp
from jax import lax
from jax.experimental import pallas as pl
from jax.experimental.pallas import tpu as pltpu
from jax.sharding import PartitionSpec as P

LOW = -1e30
FLOOR = -1e29
MESH = pl.DeviceIdType.MESH
GROUPS = 8
SIZE = 32 // GROUPS
AHEAD = 4
FEED_LAG = 3
GIVE_LAG = 6
BF = jnp.bfloat16
F32 = jnp.float32


def dot(a, b):
    return jnp.dot(a, b, preferred_element_type=F32)


def dot_tn(a, b):
    return lax.dot_general(a, b, (((0,), (0,)), ((), ())), preferred_element_type=F32)


def dot_nt(a, b):
    return lax.dot_general(a, b, (((1,), (1,)), ((), ())), preferred_element_type=F32)


def remote(src, dst, send, recv, **where):
    return pltpu.make_async_remote_copy(
        src_ref=src, dst_ref=dst, send_sem=send, recv_sem=recv, device_id=where, device_id_type=MESH
    )


def loop(lo, hi, body):
    def step(i, carry):
        body(i)
        return carry

    lax.fori_loop(lo, hi, step, 0)


def layer_kernel(
    group_ref, len_ref, sink_ref, slot_ref, alen_ref,
    query_ref, draft_ref, cache_ref, parents_ref, aidx_ref, wout_ref, hidden_ref, gain_ref,
    routes_ref, weight_ref, wgu_ref, wd_ref,
    out_ref, tail_ref,
    kv, qraw, qown, qin, obuf, sbuf, oin, sin, tbuf, tin, att, wout,
    hpad, zsend, zrecv, piece, gall, ssend, srecv, nq,
    wgu, wgp, wd, wdp, put, mix, sent, arrived, zout, zin, keep, back, got, gains, fsend, frecv,
    kv_sem, q_send, q_recv, o_send, o_recv, s_send, s_recv, t_sem, w_sem,
    z_send, z_recv, g_send, g_recv, n_send, n_recv,
    d_send, d_recv, f_send, f_recv, p_send, p_recv, b_send, b_recv, e_send, e_recv,
):
    me, tp = lax.axis_index("seq"), lax.axis_index("tp")
    core, chip = lax.rem(me, 2), lax.div(me, 2)
    y, x = lax.div(chip, 4), lax.rem(chip, 4)
    odd = lax.rem(tp, 2)
    row_at = [lax.rem(y + k, 4) * 8 for k in range(4)]
    col_at = [lax.rem(x + k, 4) * 2 for k in range(4)]
    core_at = [core, 1 - core]

    def static_away(d):
        k = d // 2
        return row_at[k % 4] + col_at[(k % 4 + k // 4) % 4] + core_at[d % 2]

    need = ((tp + 2) // 4) % 2

    def peer(k, sign, flip):
        step = lax.rem(k, 4)
        ny = lax.rem(y + sign * step + 4, 4)
        nx = lax.rem(x + sign * (step + lax.div(k, 4)) + 8, 4)
        return ny * 8 + nx * 2 + core_at[flip]

    def same(d, sign):
        return peer(d, sign, 0)

    barrier = pltpu.get_barrier_semaphore()

    for d in range(1, 32):
        pl.semaphore_signal(barrier, inc=1, device_id={"seq": static_away(d)}, device_id_type=MESH)
    for d in range(1, 8):
        pl.semaphore_signal(barrier, inc=1, device_id={"tp": lax.rem(tp + d, 8)}, device_id_type=MESH)

    own_half = pltpu.make_async_copy(cache_ref, kv.at[:, core], kv_sem.at[0])
    own_half.start()
    loads = [
        pltpu.make_async_copy(src, dst, w_sem.at[i])
        for i, (src, dst) in enumerate(((wout_ref, wout), (wgu_ref, wgu), (wd_ref, wd)))
    ]
    for load in loads:
        load.start()

    asked = query_ref[...].astype(F32) * 0.125
    for h in range(8):
        qraw[:, h * 64 : h * 64 + 64] = asked[:, h * 64 : h * 64 + 64].T
    query = qraw[...].astype(BF)
    qown[...] = query
    qin[0] = query
    node = lax.broadcasted_iota(jnp.int32, (64, 16), 0)
    row = lax.broadcasted_iota(jnp.int32, (64, 16), 1)
    chosen = jnp.where((node == aidx_ref[...]) & (row < alen_ref[0]), 1.0, 0.0).astype(BF)
    picked = dot_tn(chosen, draft_ref[...]).astype(BF)
    tbuf[...] = picked
    tin[me] = picked

    pl.semaphore_wait(barrier, 38)
    swap = remote(cache_ref, kv.at[:, core], kv_sem.at[1], kv_sem.at[2], seq=chip * 2 + 1 - core)
    swap.start()

    def send_query(d):
        remote(qown, qin.at[d], q_send.at[d], q_recv.at[d], seq=same(d, 1)).start()

    loop(1, 4, send_query)

    for d in range(1, 32):
        remote(tbuf, tin.at[me], t_sem.at[0], t_sem.at[1], seq=static_away(d)).start()

    draft = draft_ref[...]
    up_id = lax.broadcasted_iota(jnp.int32, (64, 64), 0)
    node_id = lax.broadcasted_iota(jnp.int32, (64, 64), 1)
    reach = jnp.where((parents_ref[...] == up_id) | (up_id == node_id), 1.0, 0.0)
    for _ in range(6):
        half = reach.astype(BF)
        reach = jnp.minimum(dot(half, half), 1.0)
    allowed = jnp.concatenate([reach] * 8, axis=1) > 0.5
    tree = jnp.where(allowed, dot(draft, jnp.concatenate([query, jnp.zeros((64, 512), BF)], axis=0)), LOW)
    tree_max = jnp.max(tree, axis=0, keepdims=True)
    tree_weight = jnp.where(allowed, jnp.exp(tree - tree_max), 0.0)
    tree_sum = jnp.sum(tree_weight, axis=0, keepdims=True)
    tree_num = dot_tn(draft, tree_weight.astype(BF))[64:]

    own_half.wait()
    swap.wait()
    position = lax.broadcasted_iota(jnp.int32, (1024, 128), 0) + chip * 1024

    def query_left(d):
        remote(qown, qin.at[d], q_send.at[d], q_recv.at[d], seq=same(d, 1)).wait_send()

    def attend(d):
        request = same(d, -1)

        @pl.when(d % 4 == 0)
        def _():
            loop(jnp.maximum(d, 1), d + 4, query_left)

            @pl.when(d < 12)
            def _():
                loop(d + 4, d + 8, send_query)

        @pl.when(d > 0)
        def _():
            remote(qown, qin.at[d], q_send.at[d], q_recv.at[d], seq=request).wait_recv()

        group = group_ref[request]
        length = len_ref[group]
        cached = kv[group].reshape(1024, 128)
        bias = jnp.where(position < length, 0.0, LOW)
        bias = jnp.concatenate([bias, bias], axis=1)
        halves = (slice(0, 256), slice(256, 512))
        scores = [
            dot(cached, jnp.concatenate([qin[d, :, cols], jnp.zeros((64, 256), BF)], axis=0)) + bias
            for cols in halves
        ]
        for cols, score in zip(halves, scores):
            top = jnp.maximum(jnp.max(score, axis=0, keepdims=True), FLOOR)
            weight = jnp.exp(score - top)
            total = jnp.sum(weight, axis=0, keepdims=True)
            value = dot_tn(cached, weight.astype(BF))[64:]
            obuf[d, :, cols] = (value / jnp.maximum(total, 1.0)).astype(BF)
            sbuf[d, 0:1, cols] = top
            sbuf[d, 1:2, cols] = total

        @pl.when(d > 0)
        def _():
            remote(obuf.at[d], oin.at[d], o_send.at[d], o_recv.at[d], seq=request).start()
            remote(sbuf.at[d], sin.at[d], s_send.at[d], s_recv.at[d], seq=request).start()

    loop(0, 16, attend)
    oin[0] = obuf[0]
    sin[0] = sbuf[0]

    expert_id = lax.broadcasted_iota(jnp.int32, (32, 64), 0)
    member = jnp.zeros((32, 64), F32)
    given = jnp.zeros((32, 64), F32)
    for k in range(4):
        hit = routes_ref[k : k + 1, :] == expert_id
        member = jnp.where(hit, 1.0, member)
        given = jnp.where(hit, weight_ref[k : k + 1, :], given)
    rank = dot(member.astype(BF), jnp.where(up_id < node_id, 1.0, 0.0).astype(BF))
    slot = lax.broadcasted_iota(jnp.int32, (16, 64), 0).astype(F32)
    for e in range(32):
        here = (slot == rank[e : e + 1, :]) & (member[e : e + 1, :] > 0.5)
        put[e * 16 : e * 16 + 16, :] = jnp.where(here, 1.0, 0.0).astype(BF)
        mix[e * 16 : e * 16 + 16, :] = jnp.where(here, given[e : e + 1, :], 0.0)
    for load in loads:
        load.wait()
    blank = jnp.zeros((360, 24), BF)
    for j in range(8):
        span, wide = slice(360 * j, 360 * j + 360), slice(384 * j, 384 * j + 384)
        wgp[0, :, wide] = jnp.concatenate([wgu[0, :, span], blank], axis=1)
        wgp[1, :, wide] = jnp.concatenate([wgu[1, :, span], blank], axis=1)
        wdp[:, wide] = jnp.concatenate([wd[:, span], blank], axis=1)
    zsend[...] = jnp.zeros((8, 64, 384), BF)
    hpad[...] = jnp.zeros((64, 384), F32)
    hpad[:, 0:360] = hidden_ref[...].astype(F32)
    gains[...] = jnp.zeros((8, 1, 384), F32)
    for j in range(8):
        gains[j, :, 0:360] = gain_ref[360 * j : 360 * j + 360].reshape(1, 360)

    lane = lax.broadcasted_iota(jnp.int32, (1, 512), 1)
    sink = jnp.zeros((1, 512), F32)
    for h in range(8):
        sink = jnp.where(lane // 64 == h, sink_ref[h], sink)

    def land(d):
        other = same(d, 1)
        remote(obuf.at[d], oin.at[d], o_send.at[d], o_recv.at[d], seq=other).wait()
        remote(sbuf.at[d], sin.at[d], s_send.at[d], s_recv.at[d], seq=other).wait()

    loop(1, 16, land)
    ceiling = jnp.maximum(tree_max, sink)
    for d in range(16):
        ceiling = jnp.maximum(ceiling, sin[d, 0:1])
    tree_scale = jnp.exp(tree_max - ceiling)
    below = tree_scale * tree_sum + jnp.exp(sink - ceiling)
    above = tree_scale * tree_num
    for d in range(16):
        scale = sin[d, 1:2] * jnp.exp(sin[d, 0:1] - ceiling)
        below = below + scale
        above = above + scale * oin[d].astype(F32)
    merged = above / below
    for h in range(8):
        att[:, h * 64 : h * 64 + 64] = merged[:, h * 64 : h * 64 + 64].T
    attended = att[...].astype(BF)
    for j in range(8):
        zsend[j, :, 0:360] = dot_nt(attended, wout[360 * j : 360 * j + 360, :]).astype(BF)

    def send_piece(d):
        to = (tp + d) % 8
        remote(zsend.at[to], zrecv.at[d], z_send.at[d], z_recv.at[d], tp=to).start()

    loop(1, 8, send_piece)
    total = hpad[...] + zsend[tp].astype(F32)
    for d in range(1, 8):
        remote(zsend.at[d], zrecv.at[d], z_send.at[d], z_recv.at[d], tp=(tp + d) % 8).wait()
        total = total + zrecv[d].astype(F32)
    stream = total.astype(BF)
    piece[...] = stream
    stream_f = stream.astype(F32)

    for k in range(4):
        to = 2 * k + need

        @pl.when(to != tp)
        def _(k=k, to=to):
            remote(piece, gall.at[tp % 4], g_send.at[k], g_recv.at[tp % 4], tp=to).start()

        @pl.when(to == tp)
        def _():
            gall[tp % 4] = piece[...]

    squares = jnp.sum(stream_f * stream_f, axis=1, keepdims=True)
    square = jnp.broadcast_to(squares, (64, 128))
    spread_rows = jnp.concatenate([square, square], axis=0).T[0:8]
    ssend[...] = spread_rows

    def send_norm(d):
        remote(ssend, srecv.at[d], n_send.at[d], n_recv.at[d], tp=(tp + d) % 8).start()

    loop(1, 8, send_norm)
    summed = spread_rows
    for d in range(1, 8):
        remote(ssend, srecv.at[d], n_send.at[d], n_recv.at[d], tp=(tp + d) % 8).wait()
        summed = summed + srecv[d]
    column = jnp.concatenate([summed] * 16, axis=0).T[0:64, 0:1]
    inverse = lax.rsqrt(column * (1.0 / 2880.0) + 1e-05)

    for k in range(4):
        source = k + 4 * ((k // 2 + odd) % 2)

        @pl.when(source != tp)
        def _(k=k, source=source):
            remote(piece, gall.at[k], g_send.at[k], g_recv.at[k], tp=source).wait_recv()

    mine = (odd, 3 - odd)
    for h in range(2):
        for i in range(2):
            j = 2 * mine[h] + i
            normed = gall[j % 4].astype(F32) * inverse * gains[j]
            nq[h, :, 384 * i : 384 * i + 384] = normed.astype(BF)

    for h in range(2):
        @pl.loop(0, 4)
        def _(b, h=h):
            rows = put[pl.ds(pl.multiple_of(b * 128, 128), 128), :]
            sent[h, pl.ds(b * 8, 8)] = dot(rows, nq[h]).astype(BF).reshape(8, 16, 768)

    def dispatch(g, first=0):
        for i in range(first, SIZE):
            to = peer(SIZE // 2 * g + i // 2, 1, i % 2)
            d = SIZE * g + i
            for h in range(2):
                remote(
                    sent.at[h, to], arrived.at[mine[h], d], d_send.at[h, g], d_recv.at[h, d], seq=to
                ).start()

    def dispatched(g, count):
        for h in range(2):
            block = sent.at[h, pl.ds(0, count)]
            pltpu.make_async_copy(block, block, d_send.at[h, g]).wait()

    dispatch(0, 1)
    for g in range(1, AHEAD):
        dispatch(g)
    for h in range(2):
        arrived[mine[h], 0] = sent[h, me]

    partner = (tp + 1 - 2 * odd, lax.rem(tp + 7 + 2 * odd, 8))
    other = (1 - odd, 2 + odd)

    def forward(g):
        for i in range(SIZE):
            d = SIZE * g + i
            for h in range(2):
                @pl.when(d > 0)
                def _(h=h, d=d):
                    remote(
                        sent.at[h, 0], arrived.at[mine[h], d], d_send.at[h, 0], d_recv.at[h, d],
                        seq=static_away(1),
                    ).wait_recv()

                block = arrived.at[mine[h], d]
                remote(block, block, f_send.at[h], f_recv.at[h, g], tp=partner[h]).start()

    def feed(g):
        for h in range(2):
            block = arrived.at[other[h], pl.ds(g * SIZE, SIZE)]
            pltpu.make_async_copy(block, block, f_recv.at[h, g]).wait()
        gate = jnp.zeros((16 * SIZE, 360), F32)
        up = jnp.zeros((16 * SIZE, 360), F32)
        for q in range(4):
            rows = arrived[q, pl.ds(g * SIZE, SIZE)].reshape(16 * SIZE, 768)
            cols = slice(768 * q, 768 * q + 768)
            gate = gate + dot_nt(rows, wgp[0, :, cols])
            up = up + dot_nt(rows, wgp[1, :, cols])
        act = (gate * jax.nn.sigmoid(1.702 * gate) * (up + 1.0)).astype(BF)
        for h in range(2):
            far = dot(act, wdp[:, pl.ds(pl.multiple_of(768 * other[h], 128), 768)])
            zout[h, g] = far.astype(BF).reshape(SIZE, 16, 768)
            remote(zout.at[h, g], zin.at[h, g], p_send.at[h, g], p_recv.at[h, g], tp=partner[h]).start()
        for h in range(2):
            keep[h, g] = dot(act, wdp[:, pl.ds(pl.multiple_of(768 * mine[h], 128), 768)])

    def give(g):
        for h in range(2):
            remote(zout.at[h, g], zin.at[h, g], p_send.at[h, g], p_recv.at[h, g], tp=partner[h]).wait()
            both = keep[h, g] + zin[h, g].reshape(16 * SIZE, 768).astype(F32)
            back[h, pl.ds(g * SIZE, SIZE)] = both.astype(BF).reshape(SIZE, 16, 768)

        for i in range(SIZE):
            to = peer(SIZE // 2 * g + i // 2, -1, i % 2)
            d = SIZE * g + i
            for h in range(2):
                @pl.when(d > 0)
                def _(h=h, d=d, to=to):
                    remote(back.at[h, d], got.at[h, me], b_send.at[h], b_recv.at[h], seq=to).start()

    def stage(i):
        @pl.when(i == 0)
        def _():
            dispatched(0, SIZE - 1)

        @pl.when((i > 0) & (i < GROUPS))
        def _():
            dispatched(i, SIZE)

        @pl.when(i < GROUPS - AHEAD)
        def _():
            dispatch(i + AHEAD)

        @pl.when(i < GROUPS)
        def _():
            forward(i)

        @pl.when((i >= FEED_LAG) & (i < GROUPS + FEED_LAG))
        def _():
            feed(i - FEED_LAG)

        @pl.when(i >= GIVE_LAG)
        def _():
            give(i - GIVE_LAG)

    loop(0, GROUPS + GIVE_LAG, stage)
    for h in range(2):
        got[h, me] = back[h, 0]

    weight = mix[...].T
    high = weight.astype(BF)
    low = (weight - high.astype(F32)).astype(BF)
    mixing = jnp.concatenate([high, low], axis=0)

    def drain(ref, sem):
        pltpu.make_async_copy(ref.at[pl.ds(0, 31)], ref.at[pl.ds(0, 31)], sem).wait()

    for h in range(2):
        drain(got.at[h], b_recv.at[h])
        both = dot(mixing, got[h].reshape(512, 768))
        both = both[0:64] + both[64:128]
        for i in range(2):
            k = 2 * h + i
            to = 2 * mine[h] + i
            fsend[k] = both[:, 384 * i : 384 * i + 384].astype(BF)

            @pl.when(to != tp)
            def _(k=k, to=to):
                remote(fsend.at[k], frecv.at[tp // 2], e_send.at[k], e_recv.at[tp // 2], tp=to).start()

            @pl.when(to == tp)
            def _(k=k):
                frecv[tp // 2] = fsend[k]

    total = piece[...].astype(F32)
    for k in range(4):
        source = 2 * k + need

        @pl.when(source != tp)
        def _(k=k, source=source):
            remote(fsend.at[k], frecv.at[k], e_send.at[k], e_recv.at[k], tp=source).wait_recv()

        total = total + frecv[k].astype(F32)
    out_ref[...] = total[:, 0:360].astype(BF)

    drain(tin, t_sem.at[0])
    drain(tin, t_sem.at[1])
    kept = jnp.zeros((16, 128), F32)
    for r in range(32):
        kept = kept + jnp.where(slot_ref[r] == me, tin[r].astype(F32), 0.0)
    tail_ref[...] = kept.astype(BF)

    for k in range(4):
        @pl.when(2 * k + need != tp)
        def _(k=k):
            remote(piece, gall.at[k], g_send.at[k], g_recv.at[k], tp=2 * k + need).wait_send()

        to = 2 * mine[k // 2] + k % 2

        @pl.when(to != tp)
        def _(k=k, to=to):
            remote(fsend.at[k], frecv.at[k], e_send.at[k], e_recv.at[k], tp=to).wait_send()

    for h in range(2):
        drain(back.at[h], b_send.at[h])
        pltpu.make_async_copy(sent.at[h], sent.at[h], f_send.at[h]).wait()


def run_layer(*operands):
    smem = pl.BlockSpec(memory_space=pltpu.SMEM)
    vmem = pl.BlockSpec(memory_space=pltpu.VMEM)
    hbm = pl.BlockSpec(memory_space=pl.ANY)
    dma = pltpu.SemaphoreType.DMA
    return pl.pallas_call(
        layer_kernel,
        out_shape=(jax.ShapeDtypeStruct((64, 360), BF), jax.ShapeDtypeStruct((16, 128), BF)),
        in_specs=[smem] * 5 + [vmem, vmem, hbm, vmem, vmem, hbm, vmem, vmem, vmem, vmem, hbm, hbm],
        out_specs=(vmem, vmem),
        scratch_shapes=[
            pltpu.VMEM((8, 2, 512, 128), BF),
            pltpu.VMEM((64, 512), F32),
            pltpu.VMEM((64, 512), BF),
            pltpu.VMEM((16, 64, 512), BF),
            pltpu.VMEM((16, 64, 512), BF),
            pltpu.VMEM((16, 2, 512), F32),
            pltpu.VMEM((16, 64, 512), BF),
            pltpu.VMEM((16, 2, 512), F32),
            pltpu.VMEM((16, 128), BF),
            pltpu.VMEM((32, 16, 128), BF),
            pltpu.VMEM((64, 512), F32),
            pltpu.VMEM((2880, 512), BF),
            pltpu.VMEM((64, 384), F32),
            pltpu.VMEM((8, 64, 384), BF),
            pltpu.VMEM((8, 64, 384), BF),
            pltpu.VMEM((64, 384), BF),
            pltpu.VMEM((4, 64, 384), BF),
            pltpu.VMEM((8, 128), F32),
            pltpu.VMEM((8, 8, 128), F32),
            pltpu.VMEM((2, 64, 768), BF),
            pltpu.VMEM((2, 360, 2880), BF),
            pltpu.VMEM((2, 360, 3072), BF),
            pltpu.VMEM((360, 2880), BF),
            pltpu.VMEM((360, 3072), BF),
            pltpu.VMEM((512, 64), BF),
            pltpu.VMEM((512, 64), F32),
            pltpu.VMEM((2, 32, 16, 768), BF),
            pltpu.VMEM((4, 32, 16, 768), BF),
            pltpu.VMEM((2, GROUPS, SIZE, 16, 768), BF),
            pltpu.VMEM((2, GROUPS, SIZE, 16, 768), BF),
            pltpu.VMEM((2, GROUPS, 16 * SIZE, 768), F32),
            pltpu.VMEM((2, 32, 16, 768), BF),
            pltpu.VMEM((2, 32, 16, 768), BF),
            pltpu.VMEM((8, 1, 384), F32),
            pltpu.VMEM((4, 64, 384), BF),
            pltpu.VMEM((4, 64, 384), BF),
            dma((3,)), dma((16,)), dma((16,)), dma((16,)), dma((16,)), dma((16,)), dma((16,)),
            dma((2,)), dma((3,)),
            dma((8,)), dma((8,)), dma((4,)), dma((4,)), dma((8,)), dma((8,)),
            dma((2, GROUPS)), dma((2, 32)), dma((2,)), dma((2, GROUPS)), dma((2, GROUPS)), dma((2, GROUPS)),
            dma((2,)), dma((2,)), dma((4,)), dma((4,)),
        ],
        compiler_params=pltpu.CompilerParams(
            collective_id=0, has_side_effects=True, vmem_limit_bytes=62 * 1024 * 1024
        ),
        name="layer",
    )(*operands)


def hand_over_kernel(out_ref, tail_ref, out_to, tail_to):
    out_to[...] = out_ref[...]
    tail_to[...] = tail_ref[...]


def hand_over(out, tail):
    vmem = pl.BlockSpec(memory_space=pltpu.VMEM)
    return pl.pallas_call(
        hand_over_kernel,
        out_shape=(jax.ShapeDtypeStruct(out.shape, BF), jax.ShapeDtypeStruct(tail.shape, BF)),
        in_specs=[vmem, vmem],
        out_specs=(vmem, vmem),
        name="hand_over",
    )(out, tail)


def shards(
    queries, draft_kv, cache_kv, cache_len, group_of, parents, sink_logit, w_out, hidden_in,
    norm_gain, routes, route_weight, w_gate_up, w_down, accepted_idx, accepted_len, tail_slot,
):
    out, tail = run_layer(
        group_of, cache_len, sink_logit, tail_slot, accepted_len,
        queries.reshape(64, 512), draft_kv.reshape(64, 128), cache_kv.reshape(8, 512, 128), parents,
        accepted_idx, w_out.T, hidden_in, norm_gain, routes.T, route_weight.T,
        w_gate_up.reshape(2, 2880, 360).transpose(0, 2, 1), w_down.reshape(360, 2880),
    )
    out, tail = hand_over(out, tail)
    return (out, tail.reshape(1, 16, 1, 128))


def solution(mesh):
    in_specs = (
        P("seq", None, "tp"),
        P("seq", None, "tp", None),
        P(None, "seq", "tp", None),
        P(),
        P(),
        P("seq", None),
        P("tp"),
        P("tp", None),
        P("seq", "tp"),
        P(),
        P("seq", None),
        P("seq", None),
        P("seq", None, None, "tp"),
        P("seq", "tp", None),
        P("seq", None),
        P("seq"),
        P(),
    )
    out_specs = (P("seq", "tp"), P("seq", None, "tp", None))
    return jax.shard_map(shards, mesh=mesh, in_specs=in_specs, out_specs=out_specs, check_vma=False)
```

```python
import jax
import jax.numpy as jnp
from jax import lax
from jax.experimental import pallas as pl
from jax.experimental.pallas import tpu as pltpu
from jax.sharding import PartitionSpec as P

LOW = -1e30
FLOOR = -1e29
MESH = pl.DeviceIdType.MESH
GROUPS = 8
SIZE = 32 // GROUPS
AHEAD = 4
FEED_LAG = 3
GIVE_LAG = 6
BF = jnp.bfloat16
F32 = jnp.float32


def dot(a, b):
    return jnp.dot(a, b, preferred_element_type=F32)


def dot_tn(a, b):
    return lax.dot_general(a, b, (((0,), (0,)), ((), ())), preferred_element_type=F32)


def dot_nt(a, b):
    return lax.dot_general(a, b, (((1,), (1,)), ((), ())), preferred_element_type=F32)


def remote(src, dst, send, recv, **where):
    return pltpu.make_async_remote_copy(
        src_ref=src, dst_ref=dst, send_sem=send, recv_sem=recv, device_id=where, device_id_type=MESH
    )


def loop(lo, hi, body):
    def step(i, carry):
        body(i)
        return carry

    lax.fori_loop(lo, hi, step, 0)


def layer_kernel(
    group_ref, len_ref, sink_ref, slot_ref, alen_ref,
    query_ref, draft_ref, cache_ref, parents_ref, aidx_ref, wout_ref, hidden_ref, gain_ref,
    routes_ref, weight_ref, wgu_ref, wd_ref,
    out_ref, tail_ref,
    kv, qraw, qown, qin, obuf, sbuf, oin, sin, tbuf, tin, att, wout,
    hpad, zsend, zrecv, piece, gall, ssend, srecv, nq,
    wgu, wgp, wd, wdp, put, mix, sent, arrived, zout, zin, keep, back, got, gains, fsend, frecv,
    kv_sem, q_send, q_recv, h_send, h_recv, o_send, o_recv, s_send, s_recv, t_sem, w_sem,
    z_send, z_recv, g_send, g_recv, n_send, n_recv,
    d_send, d_recv, f_send, f_recv, p_send, p_recv, b_send, b_recv, e_send, e_recv,
):
    me, tp = lax.axis_index("seq"), lax.axis_index("tp")
    core, chip = lax.rem(me, 2), lax.div(me, 2)
    y, x = lax.div(chip, 4), lax.rem(chip, 4)
    odd = lax.rem(tp, 2)
    row_at = [lax.rem(y + k, 4) * 8 for k in range(4)]
    col_at = [lax.rem(x + k, 4) * 2 for k in range(4)]
    core_at = [core, 1 - core]

    def static_away(d):
        k = d // 2
        return row_at[k % 4] + col_at[(k % 4 + k // 4) % 4] + core_at[d % 2]

    need = ((tp + 2) // 4) % 2

    def peer(k, sign, flip):
        step = lax.rem(k, 4)
        ny = lax.rem(y + sign * step + 4, 4)
        nx = lax.rem(x + sign * (step + lax.div(k, 4)) + 8, 4)
        return ny * 8 + nx * 2 + core_at[flip]

    def same(n, sign):
        corner = n - 7
        dy = jnp.where(n < 4, 0, jnp.where(n < 7, n - 3, 1 + lax.div(jnp.maximum(corner, 0), 3)))
        dx = jnp.where(n < 4, n, jnp.where(n < 7, 0, 1 + lax.rem(jnp.maximum(corner, 0), 3)))
        ny = lax.rem(y + sign * dy + 4, 4)
        nx = lax.rem(x + sign * dx + 4, 4)
        return ny * 8 + nx * 2 + core

    barrier = pltpu.get_barrier_semaphore()

    for d in range(1, 32):
        pl.semaphore_signal(barrier, inc=1, device_id={"seq": static_away(d)}, device_id_type=MESH)
    for d in range(1, 8):
        pl.semaphore_signal(barrier, inc=1, device_id={"tp": lax.rem(tp + d, 8)}, device_id_type=MESH)

    own_half = pltpu.make_async_copy(cache_ref, kv.at[:, core], kv_sem.at[0])
    own_half.start()
    loads = [
        pltpu.make_async_copy(src, dst, w_sem.at[i])
        for i, (src, dst) in enumerate(((wout_ref, wout), (wgu_ref, wgu), (wd_ref, wd)))
    ]
    for load in loads:
        load.start()

    asked = query_ref[...].astype(F32) * 0.125
    for h in range(8):
        qraw[:, h * 64 : h * 64 + 64] = asked[:, h * 64 : h * 64 + 64].T
    query = qraw[...].astype(BF)
    qown[...] = query
    qin[0] = query
    node = lax.broadcasted_iota(jnp.int32, (64, 16), 0)
    row = lax.broadcasted_iota(jnp.int32, (64, 16), 1)
    chosen = jnp.where((node == aidx_ref[...]) & (row < alen_ref[0]), 1.0, 0.0).astype(BF)
    picked = dot_tn(chosen, draft_ref[...]).astype(BF)
    tbuf[...] = picked
    tin[me] = picked

    pl.semaphore_wait(barrier, 38)
    swap = remote(cache_ref, kv.at[:, core], kv_sem.at[1], kv_sem.at[2], seq=chip * 2 + 1 - core)
    swap.start()

    def along(k):
        return row_at[0] + col_at[k] + core if k < 4 else row_at[k - 3] + col_at[0] + core

    def first_query(k):
        return remote(qown, qin.at[k], q_send.at[k], q_recv.at[k], seq=along(k))

    def relayed(axis, a, b):
        dy, dx = (b, a) if axis == 0 else (a, b)
        held, slot = (dx, 7 + 3 * (dy - 1) + dx - 1) if axis == 0 else (3 + dy, 7 + 3 * (dy - 1) + dx - 1)
        half = pl.ds(32 * axis, 32)
        return remote(
            qin.at[held, half], qin.at[slot, half], h_send.at[axis, slot], h_recv.at[axis, slot],
            seq=along(3 + b) if axis == 0 else along(b),
        )

    for k in range(1, 4):
        first_query(k).start()
        first_query(3 + k).start()
    for d in range(1, 32):
        remote(tbuf, tin.at[me], t_sem.at[0], t_sem.at[1], seq=static_away(d)).start()

    draft = draft_ref[...]
    up_id = lax.broadcasted_iota(jnp.int32, (64, 64), 0)
    node_id = lax.broadcasted_iota(jnp.int32, (64, 64), 1)
    reach = jnp.where((parents_ref[...] == up_id) | (up_id == node_id), 1.0, 0.0)
    for _ in range(6):
        half = reach.astype(BF)
        reach = jnp.minimum(dot(half, half), 1.0)
    allowed = jnp.concatenate([reach] * 8, axis=1) > 0.5
    tree = jnp.where(allowed, dot(draft, jnp.concatenate([query, jnp.zeros((64, 512), BF)], axis=0)), LOW)
    tree_max = jnp.max(tree, axis=0, keepdims=True)
    tree_weight = jnp.where(allowed, jnp.exp(tree - tree_max), 0.0)
    tree_sum = jnp.sum(tree_weight, axis=0, keepdims=True)
    tree_num = dot_tn(draft, tree_weight.astype(BF))[64:]

    expert_id = lax.broadcasted_iota(jnp.int32, (32, 64), 0)
    member = jnp.zeros((32, 64), F32)
    given = jnp.zeros((32, 64), F32)
    for k in range(4):
        hit = routes_ref[k : k + 1, :] == expert_id
        member = jnp.where(hit, 1.0, member)
        given = jnp.where(hit, weight_ref[k : k + 1, :], given)
    rank = dot(member.astype(BF), jnp.where(up_id < node_id, 1.0, 0.0).astype(BF))
    slot = lax.broadcasted_iota(jnp.int32, (16, 64), 0).astype(F32)
    for e in range(32):
        here = (slot == rank[e : e + 1, :]) & (member[e : e + 1, :] > 0.5)
        put[e * 16 : e * 16 + 16, :] = jnp.where(here, 1.0, 0.0).astype(BF)
        mix[e * 16 : e * 16 + 16, :] = jnp.where(here, given[e : e + 1, :], 0.0)
    for load in loads:
        load.wait()
    blank = jnp.zeros((360, 24), BF)
    for j in range(8):
        span, wide = slice(360 * j, 360 * j + 360), slice(384 * j, 384 * j + 384)
        wgp[0, :, wide] = jnp.concatenate([wgu[0, :, span], blank], axis=1)
        wgp[1, :, wide] = jnp.concatenate([wgu[1, :, span], blank], axis=1)
        wdp[:, wide] = jnp.concatenate([wd[:, span], blank], axis=1)
    zsend[...] = jnp.zeros((8, 64, 384), BF)
    hpad[...] = jnp.zeros((64, 384), F32)
    hpad[:, 0:360] = hidden_ref[...].astype(F32)
    gains[...] = jnp.zeros((8, 1, 384), F32)
    for j in range(8):
        gains[j, :, 0:360] = gain_ref[360 * j : 360 * j + 360].reshape(1, 360)

    own_half.wait()
    swap.wait()
    position = lax.broadcasted_iota(jnp.int32, (1024, 128), 0) + chip * 1024

    def attend(d):
        request = same(d, -1)

        @pl.when(d == 1)
        def _():
            for a in range(1, 4):
                for axis in range(2):
                    first_query(a + 3 * axis).wait_recv()
                    for b in range(1, 4):
                        relayed(axis, a, b).start()

        @pl.when(d > 6)
        def _():
            for axis in range(2):
                half = pl.ds(32 * axis, 32)
                remote(
                    qown.at[half], qin.at[d, half], h_send.at[axis, 0], h_recv.at[axis, d], seq=request
                ).wait_recv()

        group = group_ref[request]
        length = len_ref[group]
        cached = kv[group].reshape(1024, 128)
        bias = jnp.where(position < length, 0.0, LOW)
        bias = jnp.concatenate([bias, bias], axis=1)
        halves = (slice(0, 256), slice(256, 512))
        scores = [
            dot(cached, jnp.concatenate([qin[d, :, cols], jnp.zeros((64, 256), BF)], axis=0)) + bias
            for cols in halves
        ]
        for cols, score in zip(halves, scores):
            top = jnp.maximum(jnp.max(score, axis=0, keepdims=True), FLOOR)
            weight = jnp.exp(score - top)
            total = jnp.sum(weight, axis=0, keepdims=True)
            value = dot_tn(cached, weight.astype(BF))[64:]
            obuf[d, :, cols] = (value / jnp.maximum(total, 1.0)).astype(BF)
            sbuf[d, 0:1, cols] = top
            sbuf[d, 1:2, cols] = total

        @pl.when(d > 0)
        def _():
            remote(obuf.at[d], oin.at[d], o_send.at[d], o_recv.at[d], seq=request).start()
            remote(sbuf.at[d], sin.at[d], s_send.at[d], s_recv.at[d], seq=request).start()

    loop(0, 16, attend)
    oin[0] = obuf[0]
    sin[0] = sbuf[0]

    lane = lax.broadcasted_iota(jnp.int32, (1, 512), 1)
    sink = jnp.zeros((1, 512), F32)
    for h in range(8):
        sink = jnp.where(lane // 64 == h, sink_ref[h], sink)

    def land(d):
        other = same(d, 1)
        remote(obuf.at[d], oin.at[d], o_send.at[d], o_recv.at[d], seq=other).wait()
        remote(sbuf.at[d], sin.at[d], s_send.at[d], s_recv.at[d], seq=other).wait()

    loop(1, 16, land)
    for a in range(1, 4):
        for axis in range(2):
            first_query(a + 3 * axis).wait_send()
            for b in range(1, 4):
                relayed(axis, a, b).wait_send()
    ceiling = jnp.maximum(tree_max, sink)
    for d in range(16):
        ceiling = jnp.maximum(ceiling, sin[d, 0:1])
    tree_scale = jnp.exp(tree_max - ceiling)
    below = tree_scale * tree_sum + jnp.exp(sink - ceiling)
    above = tree_scale * tree_num
    for d in range(16):
        scale = sin[d, 1:2] * jnp.exp(sin[d, 0:1] - ceiling)
        below = below + scale
        above = above + scale * oin[d].astype(F32)
    merged = above / below
    for h in range(8):
        att[:, h * 64 : h * 64 + 64] = merged[:, h * 64 : h * 64 + 64].T
    attended = att[...].astype(BF)
    for j in range(8):
        zsend[j, :, 0:360] = dot_nt(attended, wout[360 * j : 360 * j + 360, :]).astype(BF)

    def send_piece(d):
        to = (tp + d) % 8
        remote(zsend.at[to], zrecv.at[d], z_send.at[d], z_recv.at[d], tp=to).start()

    loop(1, 8, send_piece)
    total = hpad[...] + zsend[tp].astype(F32)
    for d in range(1, 8):
        remote(zsend.at[d], zrecv.at[d], z_send.at[d], z_recv.at[d], tp=(tp + d) % 8).wait()
        total = total + zrecv[d].astype(F32)
    stream = total.astype(BF)
    piece[...] = stream
    stream_f = stream.astype(F32)

    for k in range(4):
        to = 2 * k + need

        @pl.when(to != tp)
        def _(k=k, to=to):
            remote(piece, gall.at[tp % 4], g_send.at[k], g_recv.at[tp % 4], tp=to).start()

        @pl.when(to == tp)
        def _():
            gall[tp % 4] = piece[...]

    squares = jnp.sum(stream_f * stream_f, axis=1, keepdims=True)
    square = jnp.broadcast_to(squares, (64, 128))
    spread_rows = jnp.concatenate([square, square], axis=0).T[0:8]
    ssend[...] = spread_rows

    def send_norm(d):
        remote(ssend, srecv.at[d], n_send.at[d], n_recv.at[d], tp=(tp + d) % 8).start()

    loop(1, 8, send_norm)
    summed = spread_rows
    for d in range(1, 8):
        remote(ssend, srecv.at[d], n_send.at[d], n_recv.at[d], tp=(tp + d) % 8).wait()
        summed = summed + srecv[d]
    column = jnp.concatenate([summed] * 16, axis=0).T[0:64, 0:1]
    inverse = lax.rsqrt(column * (1.0 / 2880.0) + 1e-05)

    for k in range(4):
        source = k + 4 * ((k // 2 + odd) % 2)

        @pl.when(source != tp)
        def _(k=k, source=source):
            remote(piece, gall.at[k], g_send.at[k], g_recv.at[k], tp=source).wait_recv()

    mine = (odd, 3 - odd)
    for h in range(2):
        for i in range(2):
            j = 2 * mine[h] + i
            normed = gall[j % 4].astype(F32) * inverse * gains[j]
            nq[h, :, 384 * i : 384 * i + 384] = normed.astype(BF)

    for h in range(2):
        @pl.loop(0, 4)
        def _(b, h=h):
            rows = put[pl.ds(pl.multiple_of(b * 128, 128), 128), :]
            sent[h, pl.ds(b * 8, 8)] = dot(rows, nq[h]).astype(BF).reshape(8, 16, 768)

    def dispatch(g, first=0):
        for i in range(first, SIZE):
            to = peer(SIZE // 2 * g + i // 2, 1, i % 2)
            d = SIZE * g + i
            for h in range(2):
                remote(
                    sent.at[h, to], arrived.at[mine[h], d], d_send.at[h, g], d_recv.at[h, d], seq=to
                ).start()

    def dispatched(g, count):
        for h in range(2):
            block = sent.at[h, pl.ds(0, count)]
            pltpu.make_async_copy(block, block, d_send.at[h, g]).wait()

    dispatch(0, 1)
    for g in range(1, AHEAD):
        dispatch(g)
    for h in range(2):
        arrived[mine[h], 0] = sent[h, me]

    partner = (tp + 1 - 2 * odd, lax.rem(tp + 7 + 2 * odd, 8))
    other = (1 - odd, 2 + odd)

    def forward(g):
        for i in range(SIZE):
            d = SIZE * g + i
            for h in range(2):
                @pl.when(d > 0)
                def _(h=h, d=d):
                    remote(
                        sent.at[h, 0], arrived.at[mine[h], d], d_send.at[h, 0], d_recv.at[h, d],
                        seq=static_away(1),
                    ).wait_recv()

                block = arrived.at[mine[h], d]
                remote(block, block, f_send.at[h], f_recv.at[h, g], tp=partner[h]).start()

    def feed(g):
        for h in range(2):
            block = arrived.at[other[h], pl.ds(g * SIZE, SIZE)]
            pltpu.make_async_copy(block, block, f_recv.at[h, g]).wait()
        gate = jnp.zeros((16 * SIZE, 360), F32)
        up = jnp.zeros((16 * SIZE, 360), F32)
        for q in range(4):
            rows = arrived[q, pl.ds(g * SIZE, SIZE)].reshape(16 * SIZE, 768)
            cols = slice(768 * q, 768 * q + 768)
            gate = gate + dot_nt(rows, wgp[0, :, cols])
            up = up + dot_nt(rows, wgp[1, :, cols])
        act = (gate * jax.nn.sigmoid(1.702 * gate) * (up + 1.0)).astype(BF)
        for h in range(2):
            far = dot(act, wdp[:, pl.ds(pl.multiple_of(768 * other[h], 128), 768)])
            zout[h, g] = far.astype(BF).reshape(SIZE, 16, 768)
            remote(zout.at[h, g], zin.at[h, g], p_send.at[h, g], p_recv.at[h, g], tp=partner[h]).start()
        for h in range(2):
            keep[h, g] = dot(act, wdp[:, pl.ds(pl.multiple_of(768 * mine[h], 128), 768)])

    def give(g):
        for h in range(2):
            remote(zout.at[h, g], zin.at[h, g], p_send.at[h, g], p_recv.at[h, g], tp=partner[h]).wait()
            both = keep[h, g] + zin[h, g].reshape(16 * SIZE, 768).astype(F32)
            back[h, pl.ds(g * SIZE, SIZE)] = both.astype(BF).reshape(SIZE, 16, 768)

        for i in range(SIZE):
            to = peer(SIZE // 2 * g + i // 2, -1, i % 2)
            d = SIZE * g + i
            for h in range(2):
                @pl.when(d > 0)
                def _(h=h, d=d, to=to):
                    remote(back.at[h, d], got.at[h, me], b_send.at[h], b_recv.at[h], seq=to).start()

    def stage(i):
        @pl.when(i == 0)
        def _():
            dispatched(0, SIZE - 1)

        @pl.when((i > 0) & (i < GROUPS))
        def _():
            dispatched(i, SIZE)

        @pl.when(i < GROUPS - AHEAD)
        def _():
            dispatch(i + AHEAD)

        @pl.when(i < GROUPS)
        def _():
            forward(i)

        @pl.when((i >= FEED_LAG) & (i < GROUPS + FEED_LAG))
        def _():
            feed(i - FEED_LAG)

        @pl.when(i >= GIVE_LAG)
        def _():
            give(i - GIVE_LAG)

    loop(0, GROUPS + GIVE_LAG, stage)
    for h in range(2):
        got[h, me] = back[h, 0]

    weight = mix[...].T
    high = weight.astype(BF)
    low = (weight - high.astype(F32)).astype(BF)
    mixing = jnp.concatenate([high, low], axis=0)

    def drain(ref, sem):
        pltpu.make_async_copy(ref.at[pl.ds(0, 31)], ref.at[pl.ds(0, 31)], sem).wait()

    for h in range(2):
        drain(got.at[h], b_recv.at[h])
        both = dot(mixing, got[h].reshape(512, 768))
        both = both[0:64] + both[64:128]
        for i in range(2):
            k = 2 * h + i
            to = 2 * mine[h] + i
            fsend[k] = both[:, 384 * i : 384 * i + 384].astype(BF)

            @pl.when(to != tp)
            def _(k=k, to=to):
                remote(fsend.at[k], frecv.at[tp // 2], e_send.at[k], e_recv.at[tp // 2], tp=to).start()

            @pl.when(to == tp)
            def _(k=k):
                frecv[tp // 2] = fsend[k]

    total = piece[...].astype(F32)
    for k in range(4):
        source = 2 * k + need

        @pl.when(source != tp)
        def _(k=k, source=source):
            remote(fsend.at[k], frecv.at[k], e_send.at[k], e_recv.at[k], tp=source).wait_recv()

        total = total + frecv[k].astype(F32)
    out_ref[...] = total[:, 0:360].astype(BF)

    drain(tin, t_sem.at[0])
    drain(tin, t_sem.at[1])
    kept = jnp.zeros((16, 128), F32)
    for r in range(32):
        kept = kept + jnp.where(slot_ref[r] == me, tin[r].astype(F32), 0.0)
    tail_ref[...] = kept.astype(BF)

    for k in range(4):
        @pl.when(2 * k + need != tp)
        def _(k=k):
            remote(piece, gall.at[k], g_send.at[k], g_recv.at[k], tp=2 * k + need).wait_send()

        to = 2 * mine[k // 2] + k % 2

        @pl.when(to != tp)
        def _(k=k, to=to):
            remote(fsend.at[k], frecv.at[k], e_send.at[k], e_recv.at[k], tp=to).wait_send()

    for h in range(2):
        drain(back.at[h], b_send.at[h])
        pltpu.make_async_copy(sent.at[h], sent.at[h], f_send.at[h]).wait()


def run_layer(*operands):
    smem = pl.BlockSpec(memory_space=pltpu.SMEM)
    vmem = pl.BlockSpec(memory_space=pltpu.VMEM)
    hbm = pl.BlockSpec(memory_space=pl.ANY)
    dma = pltpu.SemaphoreType.DMA
    return pl.pallas_call(
        layer_kernel,
        out_shape=(jax.ShapeDtypeStruct((64, 360), BF), jax.ShapeDtypeStruct((16, 128), BF)),
        in_specs=[smem] * 5 + [vmem, vmem, hbm, vmem, vmem, hbm, vmem, vmem, vmem, vmem, hbm, hbm],
        out_specs=(vmem, vmem),
        scratch_shapes=[
            pltpu.VMEM((8, 2, 512, 128), BF),
            pltpu.VMEM((64, 512), F32),
            pltpu.VMEM((64, 512), BF),
            pltpu.VMEM((16, 64, 512), BF),
            pltpu.VMEM((16, 64, 512), BF),
            pltpu.VMEM((16, 2, 512), F32),
            pltpu.VMEM((16, 64, 512), BF),
            pltpu.VMEM((16, 2, 512), F32),
            pltpu.VMEM((16, 128), BF),
            pltpu.VMEM((32, 16, 128), BF),
            pltpu.VMEM((64, 512), F32),
            pltpu.VMEM((2880, 512), BF),
            pltpu.VMEM((64, 384), F32),
            pltpu.VMEM((8, 64, 384), BF),
            pltpu.VMEM((8, 64, 384), BF),
            pltpu.VMEM((64, 384), BF),
            pltpu.VMEM((4, 64, 384), BF),
            pltpu.VMEM((8, 128), F32),
            pltpu.VMEM((8, 8, 128), F32),
            pltpu.VMEM((2, 64, 768), BF),
            pltpu.VMEM((2, 360, 2880), BF),
            pltpu.VMEM((2, 360, 3072), BF),
            pltpu.VMEM((360, 2880), BF),
            pltpu.VMEM((360, 3072), BF),
            pltpu.VMEM((512, 64), BF),
            pltpu.VMEM((512, 64), F32),
            pltpu.VMEM((2, 32, 16, 768), BF),
            pltpu.VMEM((4, 32, 16, 768), BF),
            pltpu.VMEM((2, GROUPS, SIZE, 16, 768), BF),
            pltpu.VMEM((2, GROUPS, SIZE, 16, 768), BF),
            pltpu.VMEM((2, GROUPS, 16 * SIZE, 768), F32),
            pltpu.VMEM((2, 32, 16, 768), BF),
            pltpu.VMEM((2, 32, 16, 768), BF),
            pltpu.VMEM((8, 1, 384), F32),
            pltpu.VMEM((4, 64, 384), BF),
            pltpu.VMEM((4, 64, 384), BF),
            dma((3,)), dma((7,)), dma((7,)), dma((2, 16)), dma((2, 16)), dma((16,)), dma((16,)), dma((16,)), dma((16,)),
            dma((2,)), dma((3,)),
            dma((8,)), dma((8,)), dma((4,)), dma((4,)), dma((8,)), dma((8,)),
            dma((2, GROUPS)), dma((2, 32)), dma((2,)), dma((2, GROUPS)), dma((2, GROUPS)), dma((2, GROUPS)),
            dma((2,)), dma((2,)), dma((4,)), dma((4,)),
        ],
        compiler_params=pltpu.CompilerParams(
            collective_id=0, has_side_effects=True, vmem_limit_bytes=62 * 1024 * 1024
        ),
        name="layer",
    )(*operands)


def hand_over_kernel(out_ref, tail_ref, out_to, tail_to):
    out_to[...] = out_ref[...]
    tail_to[...] = tail_ref[...]


def hand_over(out, tail):
    vmem = pl.BlockSpec(memory_space=pltpu.VMEM)
    return pl.pallas_call(
        hand_over_kernel,
        out_shape=(jax.ShapeDtypeStruct(out.shape, BF), jax.ShapeDtypeStruct(tail.shape, BF)),
        in_specs=[vmem, vmem],
        out_specs=(vmem, vmem),
        name="hand_over",
    )(out, tail)


def shards(
    queries, draft_kv, cache_kv, cache_len, group_of, parents, sink_logit, w_out, hidden_in,
    norm_gain, routes, route_weight, w_gate_up, w_down, accepted_idx, accepted_len, tail_slot,
):
    out, tail = run_layer(
        group_of, cache_len, sink_logit, tail_slot, accepted_len,
        queries.reshape(64, 512), draft_kv.reshape(64, 128), cache_kv.reshape(8, 512, 128), parents,
        accepted_idx, w_out.T, hidden_in, norm_gain, routes.T, route_weight.T,
        w_gate_up.reshape(2, 2880, 360).transpose(0, 2, 1), w_down.reshape(360, 2880),
    )
    out, tail = hand_over(out, tail)
    return (out, tail.reshape(1, 16, 1, 128))


def solution(mesh):
    in_specs = (
        P("seq", None, "tp"),
        P("seq", None, "tp", None),
        P(None, "seq", "tp", None),
        P(),
        P(),
        P("seq", None),
        P("tp"),
        P("tp", None),
        P("seq", "tp"),
        P(),
        P("seq", None),
        P("seq", None),
        P("seq", None, None, "tp"),
        P("seq", "tp", None),
        P("seq", None),
        P("seq"),
        P(),
    )
    out_specs = (P("seq", "tp"), P("seq", None, "tp", None))
    return jax.shard_map(shards, mesh=mesh, in_specs=in_specs, out_specs=out_specs, check_vma=False)
```

```python
import jax
import jax.numpy as jnp
from jax import lax
from jax.experimental import pallas as pl
from jax.experimental.pallas import tpu as pltpu
from jax.sharding import PartitionSpec as P

LOW = -1e30
FLOOR = -1e29
MESH = pl.DeviceIdType.MESH
GROUPS = 8
SIZE = 32 // GROUPS
AHEAD = 4
FEED_LAG = 3
GIVE_LAG = 6
BF = jnp.bfloat16
F32 = jnp.float32


def dot(a, b):
    return jnp.dot(a, b, preferred_element_type=F32)


def dot_tn(a, b):
    return lax.dot_general(a, b, (((0,), (0,)), ((), ())), preferred_element_type=F32)


def dot_nt(a, b):
    return lax.dot_general(a, b, (((1,), (1,)), ((), ())), preferred_element_type=F32)


def remote(src, dst, send, recv, **where):
    return pltpu.make_async_remote_copy(
        src_ref=src, dst_ref=dst, send_sem=send, recv_sem=recv, device_id=where, device_id_type=MESH
    )


def loop(lo, hi, body):
    def step(i, carry):
        body(i)
        return carry

    lax.fori_loop(lo, hi, step, 0)


def layer_kernel(
    group_ref, len_ref, sink_ref, slot_ref, alen_ref,
    query_ref, draft_ref, cache_ref, parents_ref, aidx_ref, wout_ref, hidden_ref, gain_ref,
    routes_ref, weight_ref, wgu_ref, wd_ref,
    out_ref, tail_ref,
    kv, qraw, qown, qin, obuf, sbuf, oin, sin, tbuf, tin, att, wout,
    hpad, zsend, zrecv, piece, gall, ssend, srecv, nq,
    wgu, wgp, wd, wdp, put, mix, sent, arrived, zout, zin, keep, back, got, gains, fsend, frecv,
    kv_sem, q_send, q_recv, h_send, h_recv, o_send, o_recv, s_send, s_recv, t_sem, w_sem,
    z_send, z_recv, g_send, g_recv, n_send, n_recv,
    d_send, d_recv, f_send, f_recv, p_send, p_recv, b_send, b_recv, e_send, e_recv,
):
    me, tp = lax.axis_index("seq"), lax.axis_index("tp")
    core, chip = lax.rem(me, 2), lax.div(me, 2)
    y, x = lax.div(chip, 4), lax.rem(chip, 4)
    odd = lax.rem(tp, 2)
    row_at = [lax.rem(y + k, 4) * 8 for k in range(4)]
    col_at = [lax.rem(x + k, 4) * 2 for k in range(4)]
    core_at = [core, 1 - core]

    def static_away(d):
        k = d // 2
        return row_at[k % 4] + col_at[(k % 4 + k // 4) % 4] + core_at[d % 2]

    need = ((tp + 2) // 4) % 2

    def peer(k, sign, flip):
        step = lax.rem(k, 4)
        ny = lax.rem(y + sign * step + 4, 4)
        nx = lax.rem(x + sign * (step + lax.div(k, 4)) + 8, 4)
        return ny * 8 + nx * 2 + core_at[flip]

    def same(n, sign):
        corner = n - 7
        dy = jnp.where(n < 4, 0, jnp.where(n < 7, n - 3, 1 + lax.div(jnp.maximum(corner, 0), 3)))
        dx = jnp.where(n < 4, n, jnp.where(n < 7, 0, 1 + lax.rem(jnp.maximum(corner, 0), 3)))
        ny = lax.rem(y + sign * dy + 4, 4)
        nx = lax.rem(x + sign * dx + 4, 4)
        return ny * 8 + nx * 2 + core

    barrier = pltpu.get_barrier_semaphore()

    for d in range(1, 32):
        pl.semaphore_signal(barrier, inc=1, device_id={"seq": static_away(d)}, device_id_type=MESH)
    for d in range(1, 8):
        pl.semaphore_signal(barrier, inc=1, device_id={"tp": lax.rem(tp + d, 8)}, device_id_type=MESH)

    own_half = pltpu.make_async_copy(cache_ref, kv.at[:, core], kv_sem.at[0])
    own_half.start()
    loads = [
        pltpu.make_async_copy(src, dst, w_sem.at[i])
        for i, (src, dst) in enumerate(((wout_ref, wout), (wgu_ref, wgu), (wd_ref, wd)))
    ]
    for load in loads:
        load.start()

    asked = query_ref[...].astype(F32) * 0.125
    for h in range(8):
        qraw[:, h * 64 : h * 64 + 64] = asked[:, h * 64 : h * 64 + 64].T
    query = qraw[...].astype(BF)
    qown[...] = query
    qin[0] = query
    node = lax.broadcasted_iota(jnp.int32, (64, 16), 0)
    row = lax.broadcasted_iota(jnp.int32, (64, 16), 1)
    chosen = jnp.where((node == aidx_ref[...]) & (row < alen_ref[0]), 1.0, 0.0).astype(BF)
    picked = dot_tn(chosen, draft_ref[...]).astype(BF)
    tbuf[...] = picked
    tin[me] = picked

    pl.semaphore_wait(barrier, 38)
    swap = remote(cache_ref, kv.at[:, core], kv_sem.at[1], kv_sem.at[2], seq=chip * 2 + 1 - core)
    swap.start()

    def along(k):
        return row_at[0] + col_at[k] + core if k < 4 else row_at[k - 3] + col_at[0] + core

    def first_query(k):
        return remote(qown, qin.at[k], q_send.at[k], q_recv.at[k], seq=along(k))

    def relayed(axis, a, b):
        dy, dx = (b, a) if axis == 0 else (a, b)
        held, slot = (dx, 7 + 3 * (dy - 1) + dx - 1) if axis == 0 else (3 + dy, 7 + 3 * (dy - 1) + dx - 1)
        half = pl.ds(32 * axis, 32)
        return remote(
            qin.at[held, half], qin.at[slot, half], h_send.at[axis, slot], h_recv.at[axis, slot],
            seq=along(3 + b) if axis == 0 else along(b),
        )

    for k in range(1, 4):
        first_query(k).start()
        first_query(3 + k).start()
    for d in range(1, 32):
        remote(tbuf, tin.at[me], t_sem.at[0], t_sem.at[1], seq=static_away(d)).start()

    draft = draft_ref[...]
    up_id = lax.broadcasted_iota(jnp.int32, (64, 64), 0)
    node_id = lax.broadcasted_iota(jnp.int32, (64, 64), 1)
    reach = jnp.where((parents_ref[...] == up_id) | (up_id == node_id), 1.0, 0.0)
    for _ in range(6):
        half = reach.astype(BF)
        reach = jnp.minimum(dot(half, half), 1.0)
    allowed = jnp.concatenate([reach] * 8, axis=1) > 0.5
    tree = jnp.where(allowed, dot(draft, jnp.concatenate([query, jnp.zeros((64, 512), BF)], axis=0)), LOW)
    tree_max = jnp.max(tree, axis=0, keepdims=True)
    tree_weight = jnp.where(allowed, jnp.exp(tree - tree_max), 0.0)
    tree_sum = jnp.sum(tree_weight, axis=0, keepdims=True)
    tree_num = dot_tn(draft, tree_weight.astype(BF))[64:]

    expert_id = lax.broadcasted_iota(jnp.int32, (32, 64), 0)
    member = jnp.zeros((32, 64), F32)
    given = jnp.zeros((32, 64), F32)
    for k in range(4):
        hit = routes_ref[k : k + 1, :] == expert_id
        member = jnp.where(hit, 1.0, member)
        given = jnp.where(hit, weight_ref[k : k + 1, :], given)
    rank = dot(member.astype(BF), jnp.where(up_id < node_id, 1.0, 0.0).astype(BF))
    slot = lax.broadcasted_iota(jnp.int32, (16, 64), 0).astype(F32)
    for e in range(32):
        here = (slot == rank[e : e + 1, :]) & (member[e : e + 1, :] > 0.5)
        put[e * 16 : e * 16 + 16, :] = jnp.where(here, 1.0, 0.0).astype(BF)
        mix[e * 16 : e * 16 + 16, :] = jnp.where(here, given[e : e + 1, :], 0.0)
    for load in loads:
        load.wait()
    blank = jnp.zeros((360, 24), BF)
    for j in range(8):
        span, wide = slice(360 * j, 360 * j + 360), slice(384 * j, 384 * j + 384)
        wgp[0, :, wide] = jnp.concatenate([wgu[0, :, span], blank], axis=1)
        wgp[1, :, wide] = jnp.concatenate([wgu[1, :, span], blank], axis=1)
        wdp[:, wide] = jnp.concatenate([wd[:, span], blank], axis=1)
    zsend[...] = jnp.zeros((8, 64, 384), BF)
    hpad[...] = jnp.zeros((64, 384), F32)
    hpad[:, 0:360] = hidden_ref[...].astype(F32)
    gains[...] = jnp.zeros((8, 1, 384), F32)
    for j in range(8):
        gains[j, :, 0:360] = gain_ref[360 * j : 360 * j + 360].reshape(1, 360)

    own_half.wait()
    swap.wait()
    position = lax.broadcasted_iota(jnp.int32, (1024, 128), 0) + chip * 1024

    def attend(d):
        request = same(d, -1)

        @pl.when(d == 1)
        def _():
            for a in range(1, 4):
                for axis in range(2):
                    first_query(a + 3 * axis).wait_recv()
                    for b in range(1, 4):
                        relayed(axis, a, b).start()

        @pl.when(d > 6)
        def _():
            for axis in range(2):
                half = pl.ds(32 * axis, 32)
                remote(
                    qown.at[half], qin.at[d, half], h_send.at[axis, 0], h_recv.at[axis, d], seq=request
                ).wait_recv()

        group = group_ref[request]
        length = len_ref[group]
        cached = kv[group].reshape(1024, 128)
        bias = jnp.where(position < length, 0.0, LOW)
        bias = jnp.concatenate([bias, bias], axis=1)
        halves = (slice(0, 256), slice(256, 512))
        scores = [
            dot(cached, jnp.concatenate([qin[d, :, cols], jnp.zeros((64, 256), BF)], axis=0)) + bias
            for cols in halves
        ]
        for cols, score in zip(halves, scores):
            top = jnp.maximum(jnp.max(score, axis=0, keepdims=True), FLOOR)
            weight = jnp.exp(score - top)
            total = jnp.sum(weight, axis=0, keepdims=True)
            value = dot_tn(cached, weight.astype(BF))[64:]
            obuf[d, :, cols] = (value / jnp.maximum(total, 1.0)).astype(BF)
            sbuf[d, 0:1, cols] = top
            sbuf[d, 1:2, cols] = total

        @pl.when(d > 0)
        def _():
            remote(obuf.at[d], oin.at[d], o_send.at[d], o_recv.at[d], seq=request).start()
            remote(sbuf.at[d], sin.at[d], s_send.at[d], s_recv.at[d], seq=request).start()

    loop(0, 16, attend)
    oin[0] = obuf[0]
    sin[0] = sbuf[0]

    lane = lax.broadcasted_iota(jnp.int32, (1, 512), 1)
    sink = jnp.zeros((1, 512), F32)
    for h in range(8):
        sink = jnp.where(lane // 64 == h, sink_ref[h], sink)

    def land(d):
        other = same(d, 1)
        remote(obuf.at[d], oin.at[d], o_send.at[d], o_recv.at[d], seq=other).wait()
        remote(sbuf.at[d], sin.at[d], s_send.at[d], s_recv.at[d], seq=other).wait()

    ceiling = jnp.maximum(tree_max, sink)
    tree_scale = jnp.exp(tree_max - ceiling)
    below = tree_scale * tree_sum + jnp.exp(sink - ceiling)
    above = tree_scale * tree_num
    for first in range(0, 16, 4):
        loop(max(first, 1), first + 4, land)
        before = ceiling
        for d in range(first, first + 4):
            ceiling = jnp.maximum(ceiling, sin[d, 0:1])
        fade = jnp.exp(before - ceiling)
        below = below * fade
        above = above * fade
        for d in range(first, first + 4):
            scale = sin[d, 1:2] * jnp.exp(sin[d, 0:1] - ceiling)
            below = below + scale
            above = above + scale * oin[d].astype(F32)
    for a in range(1, 4):
        for axis in range(2):
            first_query(a + 3 * axis).wait_send()
            for b in range(1, 4):
                relayed(axis, a, b).wait_send()
    merged = above / below
    for h in range(8):
        att[:, h * 64 : h * 64 + 64] = merged[:, h * 64 : h * 64 + 64].T
    attended = att[...].astype(BF)
    for j in range(8):
        zsend[j, :, 0:360] = dot_nt(attended, wout[360 * j : 360 * j + 360, :]).astype(BF)

    def send_piece(d):
        to = (tp + d) % 8
        remote(zsend.at[to], zrecv.at[d], z_send.at[d], z_recv.at[d], tp=to).start()

    loop(1, 8, send_piece)
    total = hpad[...] + zsend[tp].astype(F32)
    for d in range(1, 8):
        remote(zsend.at[d], zrecv.at[d], z_send.at[d], z_recv.at[d], tp=(tp + d) % 8).wait()
        total = total + zrecv[d].astype(F32)
    stream = total.astype(BF)
    piece[...] = stream
    stream_f = stream.astype(F32)

    for k in range(4):
        to = 2 * k + need

        @pl.when(to != tp)
        def _(k=k, to=to):
            remote(piece, gall.at[tp % 4], g_send.at[k], g_recv.at[tp % 4], tp=to).start()

        @pl.when(to == tp)
        def _():
            gall[tp % 4] = piece[...]

    squares = jnp.sum(stream_f * stream_f, axis=1, keepdims=True)
    square = jnp.broadcast_to(squares, (64, 128))
    spread_rows = jnp.concatenate([square, square], axis=0).T[0:8]
    ssend[...] = spread_rows

    def send_norm(d):
        remote(ssend, srecv.at[d], n_send.at[d], n_recv.at[d], tp=(tp + d) % 8).start()

    loop(1, 8, send_norm)
    summed = spread_rows
    for d in range(1, 8):
        remote(ssend, srecv.at[d], n_send.at[d], n_recv.at[d], tp=(tp + d) % 8).wait()
        summed = summed + srecv[d]
    column = jnp.concatenate([summed] * 16, axis=0).T[0:64, 0:1]
    inverse = lax.rsqrt(column * (1.0 / 2880.0) + 1e-05)

    for k in range(4):
        source = k + 4 * ((k // 2 + odd) % 2)

        @pl.when(source != tp)
        def _(k=k, source=source):
            remote(piece, gall.at[k], g_send.at[k], g_recv.at[k], tp=source).wait_recv()

    mine = (odd, 3 - odd)
    for h in range(2):
        for i in range(2):
            j = 2 * mine[h] + i
            normed = gall[j % 4].astype(F32) * inverse * gains[j]
            nq[h, :, 384 * i : 384 * i + 384] = normed.astype(BF)

    for h in range(2):
        @pl.loop(0, 4)
        def _(b, h=h):
            rows = put[pl.ds(pl.multiple_of(b * 128, 128), 128), :]
            sent[h, pl.ds(b * 8, 8)] = dot(rows, nq[h]).astype(BF).reshape(8, 16, 768)

    def dispatch(g, first=0):
        for i in range(first, SIZE):
            to = peer(SIZE // 2 * g + i // 2, 1, i % 2)
            d = SIZE * g + i
            for h in range(2):
                remote(
                    sent.at[h, to], arrived.at[mine[h], d], d_send.at[h, g], d_recv.at[h, d], seq=to
                ).start()

    def dispatched(g, count):
        for h in range(2):
            block = sent.at[h, pl.ds(0, count)]
            pltpu.make_async_copy(block, block, d_send.at[h, g]).wait()

    dispatch(0, 1)
    for g in range(1, AHEAD):
        dispatch(g)
    for h in range(2):
        arrived[mine[h], 0] = sent[h, me]

    partner = (tp + 1 - 2 * odd, lax.rem(tp + 7 + 2 * odd, 8))
    other = (1 - odd, 2 + odd)

    def forward(g):
        for i in range(SIZE):
            d = SIZE * g + i
            for h in range(2):
                @pl.when(d > 0)
                def _(h=h, d=d):
                    remote(
                        sent.at[h, 0], arrived.at[mine[h], d], d_send.at[h, 0], d_recv.at[h, d],
                        seq=static_away(1),
                    ).wait_recv()

                block = arrived.at[mine[h], d]
                remote(block, block, f_send.at[h], f_recv.at[h, g], tp=partner[h]).start()

    def feed(g):
        for h in range(2):
            block = arrived.at[other[h], pl.ds(g * SIZE, SIZE)]
            pltpu.make_async_copy(block, block, f_recv.at[h, g]).wait()
        gate = jnp.zeros((16 * SIZE, 360), F32)
        up = jnp.zeros((16 * SIZE, 360), F32)
        for q in range(4):
            rows = arrived[q, pl.ds(g * SIZE, SIZE)].reshape(16 * SIZE, 768)
            cols = slice(768 * q, 768 * q + 768)
            gate = gate + dot_nt(rows, wgp[0, :, cols])
            up = up + dot_nt(rows, wgp[1, :, cols])
        act = (gate * jax.nn.sigmoid(1.702 * gate) * (up + 1.0)).astype(BF)
        for h in range(2):
            far = dot(act, wdp[:, pl.ds(pl.multiple_of(768 * other[h], 128), 768)])
            zout[h, g] = far.astype(BF).reshape(SIZE, 16, 768)
            remote(zout.at[h, g], zin.at[h, g], p_send.at[h, g], p_recv.at[h, g], tp=partner[h]).start()
        for h in range(2):
            keep[h, g] = dot(act, wdp[:, pl.ds(pl.multiple_of(768 * mine[h], 128), 768)])

    def give(g):
        for h in range(2):
            remote(zout.at[h, g], zin.at[h, g], p_send.at[h, g], p_recv.at[h, g], tp=partner[h]).wait()
            both = keep[h, g] + zin[h, g].reshape(16 * SIZE, 768).astype(F32)
            back[h, pl.ds(g * SIZE, SIZE)] = both.astype(BF).reshape(SIZE, 16, 768)

        for i in range(SIZE):
            to = peer(SIZE // 2 * g + i // 2, -1, i % 2)
            d = SIZE * g + i
            for h in range(2):
                @pl.when(d > 0)
                def _(h=h, d=d, to=to):
                    remote(back.at[h, d], got.at[h, me], b_send.at[h], b_recv.at[h], seq=to).start()

    def stage(i):
        @pl.when(i == 0)
        def _():
            dispatched(0, SIZE - 1)

        @pl.when((i > 0) & (i < GROUPS))
        def _():
            dispatched(i, SIZE)

        @pl.when(i < GROUPS - AHEAD)
        def _():
            dispatch(i + AHEAD)

        @pl.when(i < GROUPS)
        def _():
            forward(i)

        @pl.when((i >= FEED_LAG) & (i < GROUPS + FEED_LAG))
        def _():
            feed(i - FEED_LAG)

        @pl.when(i >= GIVE_LAG)
        def _():
            give(i - GIVE_LAG)

    loop(0, GROUPS + GIVE_LAG, stage)
    for h in range(2):
        got[h, me] = back[h, 0]

    weight = mix[...].T
    high = weight.astype(BF)
    low = (weight - high.astype(F32)).astype(BF)
    mixing = jnp.concatenate([high, low], axis=0)

    def drain(ref, sem):
        pltpu.make_async_copy(ref.at[pl.ds(0, 31)], ref.at[pl.ds(0, 31)], sem).wait()

    for h in range(2):
        drain(got.at[h], b_recv.at[h])
        both = dot(mixing, got[h].reshape(512, 768))
        both = both[0:64] + both[64:128]
        for i in range(2):
            k = 2 * h + i
            to = 2 * mine[h] + i
            fsend[k] = both[:, 384 * i : 384 * i + 384].astype(BF)

            @pl.when(to != tp)
            def _(k=k, to=to):
                remote(fsend.at[k], frecv.at[tp // 2], e_send.at[k], e_recv.at[tp // 2], tp=to).start()

            @pl.when(to == tp)
            def _(k=k):
                frecv[tp // 2] = fsend[k]

    total = piece[...].astype(F32)
    for k in range(4):
        source = 2 * k + need

        @pl.when(source != tp)
        def _(k=k, source=source):
            remote(fsend.at[k], frecv.at[k], e_send.at[k], e_recv.at[k], tp=source).wait_recv()

        total = total + frecv[k].astype(F32)
    out_ref[...] = total[:, 0:360].astype(BF)

    drain(tin, t_sem.at[0])
    drain(tin, t_sem.at[1])
    kept = jnp.zeros((16, 128), F32)
    for r in range(32):
        kept = kept + jnp.where(slot_ref[r] == me, tin[r].astype(F32), 0.0)
    tail_ref[...] = kept.astype(BF)

    for k in range(4):
        @pl.when(2 * k + need != tp)
        def _(k=k):
            remote(piece, gall.at[k], g_send.at[k], g_recv.at[k], tp=2 * k + need).wait_send()

        to = 2 * mine[k // 2] + k % 2

        @pl.when(to != tp)
        def _(k=k, to=to):
            remote(fsend.at[k], frecv.at[k], e_send.at[k], e_recv.at[k], tp=to).wait_send()

    for h in range(2):
        drain(back.at[h], b_send.at[h])
        pltpu.make_async_copy(sent.at[h], sent.at[h], f_send.at[h]).wait()


def run_layer(*operands):
    smem = pl.BlockSpec(memory_space=pltpu.SMEM)
    vmem = pl.BlockSpec(memory_space=pltpu.VMEM)
    hbm = pl.BlockSpec(memory_space=pl.ANY)
    dma = pltpu.SemaphoreType.DMA
    return pl.pallas_call(
        layer_kernel,
        out_shape=(jax.ShapeDtypeStruct((64, 360), BF), jax.ShapeDtypeStruct((16, 128), BF)),
        in_specs=[smem] * 5 + [vmem, vmem, hbm, vmem, vmem, hbm, vmem, vmem, vmem, vmem, hbm, hbm],
        out_specs=(vmem, vmem),
        scratch_shapes=[
            pltpu.VMEM((8, 2, 512, 128), BF),
            pltpu.VMEM((64, 512), F32),
            pltpu.VMEM((64, 512), BF),
            pltpu.VMEM((16, 64, 512), BF),
            pltpu.VMEM((16, 64, 512), BF),
            pltpu.VMEM((16, 2, 512), F32),
            pltpu.VMEM((16, 64, 512), BF),
            pltpu.VMEM((16, 2, 512), F32),
            pltpu.VMEM((16, 128), BF),
            pltpu.VMEM((32, 16, 128), BF),
            pltpu.VMEM((64, 512), F32),
            pltpu.VMEM((2880, 512), BF),
            pltpu.VMEM((64, 384), F32),
            pltpu.VMEM((8, 64, 384), BF),
            pltpu.VMEM((8, 64, 384), BF),
            pltpu.VMEM((64, 384), BF),
            pltpu.VMEM((4, 64, 384), BF),
            pltpu.VMEM((8, 128), F32),
            pltpu.VMEM((8, 8, 128), F32),
            pltpu.VMEM((2, 64, 768), BF),
            pltpu.VMEM((2, 360, 2880), BF),
            pltpu.VMEM((2, 360, 3072), BF),
            pltpu.VMEM((360, 2880), BF),
            pltpu.VMEM((360, 3072), BF),
            pltpu.VMEM((512, 64), BF),
            pltpu.VMEM((512, 64), F32),
            pltpu.VMEM((2, 32, 16, 768), BF),
            pltpu.VMEM((4, 32, 16, 768), BF),
            pltpu.VMEM((2, GROUPS, SIZE, 16, 768), BF),
            pltpu.VMEM((2, GROUPS, SIZE, 16, 768), BF),
            pltpu.VMEM((2, GROUPS, 16 * SIZE, 768), F32),
            pltpu.VMEM((2, 32, 16, 768), BF),
            pltpu.VMEM((2, 32, 16, 768), BF),
            pltpu.VMEM((8, 1, 384), F32),
            pltpu.VMEM((4, 64, 384), BF),
            pltpu.VMEM((4, 64, 384), BF),
            dma((3,)), dma((7,)), dma((7,)), dma((2, 16)), dma((2, 16)), dma((16,)), dma((16,)), dma((16,)), dma((16,)),
            dma((2,)), dma((3,)),
            dma((8,)), dma((8,)), dma((4,)), dma((4,)), dma((8,)), dma((8,)),
            dma((2, GROUPS)), dma((2, 32)), dma((2,)), dma((2, GROUPS)), dma((2, GROUPS)), dma((2, GROUPS)),
            dma((2,)), dma((2,)), dma((4,)), dma((4,)),
        ],
        compiler_params=pltpu.CompilerParams(
            collective_id=0, has_side_effects=True, vmem_limit_bytes=62 * 1024 * 1024
        ),
        name="layer",
    )(*operands)


def hand_over_kernel(out_ref, tail_ref, out_to, tail_to):
    out_to[...] = out_ref[...]
    tail_to[...] = tail_ref[...]


def hand_over(out, tail):
    vmem = pl.BlockSpec(memory_space=pltpu.VMEM)
    return pl.pallas_call(
        hand_over_kernel,
        out_shape=(jax.ShapeDtypeStruct(out.shape, BF), jax.ShapeDtypeStruct(tail.shape, BF)),
        in_specs=[vmem, vmem],
        out_specs=(vmem, vmem),
        name="hand_over",
    )(out, tail)


def shards(
    queries, draft_kv, cache_kv, cache_len, group_of, parents, sink_logit, w_out, hidden_in,
    norm_gain, routes, route_weight, w_gate_up, w_down, accepted_idx, accepted_len, tail_slot,
):
    out, tail = run_layer(
        group_of, cache_len, sink_logit, tail_slot, accepted_len,
        queries.reshape(64, 512), draft_kv.reshape(64, 128), cache_kv.reshape(8, 512, 128), parents,
        accepted_idx, w_out.T, hidden_in, norm_gain, routes.T, route_weight.T,
        w_gate_up.reshape(2, 2880, 360).transpose(0, 2, 1), w_down.reshape(360, 2880),
    )
    out, tail = hand_over(out, tail)
    return (out, tail.reshape(1, 16, 1, 128))


def solution(mesh):
    in_specs = (
        P("seq", None, "tp"),
        P("seq", None, "tp", None),
        P(None, "seq", "tp", None),
        P(),
        P(),
        P("seq", None),
        P("tp"),
        P("tp", None),
        P("seq", "tp"),
        P(),
        P("seq", None),
        P("seq", None),
        P("seq", None, None, "tp"),
        P("seq", "tp", None),
        P("seq", None),
        P("seq"),
        P(),
    )
    out_specs = (P("seq", "tp"), P("seq", None, "tp", None))
    return jax.shard_map(shards, mesh=mesh, in_specs=in_specs, out_specs=out_specs, check_vma=False)
```

```python
import jax
import jax.numpy as jnp
from jax import lax
from jax.experimental import pallas as pl
from jax.experimental.pallas import tpu as pltpu
from jax.sharding import PartitionSpec as P

LOW = -1e30
FLOOR = -1e29
MESH = pl.DeviceIdType.MESH
GROUPS = 8
SIZE = 32 // GROUPS
AHEAD = 4
FEED_LAG = 3
GIVE_LAG = 6
BF = jnp.bfloat16
F32 = jnp.float32


def dot(a, b):
    return jnp.dot(a, b, preferred_element_type=F32)


def dot_tn(a, b):
    return lax.dot_general(a, b, (((0,), (0,)), ((), ())), preferred_element_type=F32)


def dot_nt(a, b):
    return lax.dot_general(a, b, (((1,), (1,)), ((), ())), preferred_element_type=F32)


def remote(src, dst, send, recv, **where):
    return pltpu.make_async_remote_copy(
        src_ref=src, dst_ref=dst, send_sem=send, recv_sem=recv, device_id=where, device_id_type=MESH
    )


def loop(lo, hi, body):
    def step(i, carry):
        body(i)
        return carry

    lax.fori_loop(lo, hi, step, 0)


def layer_kernel(
    group_ref, len_ref, sink_ref, slot_ref, alen_ref,
    query_ref, draft_ref, cache_ref, parents_ref, aidx_ref, wout_ref, hidden_ref, gain_ref,
    routes_ref, weight_ref, wgu_ref, wd_ref,
    out_ref, tail_ref,
    kv, qraw, qown, qin, obuf, sbuf, oin, sin, tbuf, tin, att, wout,
    hpad, zsend, zrecv, piece, gall, ssend, srecv, nq,
    wgu, wgp, wd, wdp, put, mix, sent, arrived, zout, zin, keep, back, got, gains, fsend, frecv,
    kv_sem, q_send, q_recv, h_send, h_recv, o_send, o_recv, s_send, s_recv, t_sem, w_sem,
    z_send, z_recv, g_send, g_recv, n_send, n_recv,
    d_send, d_recv, f_send, f_recv, p_send, p_recv, b_send, b_recv, e_send, e_recv,
):
    me, tp = lax.axis_index("seq"), lax.axis_index("tp")
    core, chip = lax.rem(me, 2), lax.div(me, 2)
    y, x = lax.div(chip, 4), lax.rem(chip, 4)
    odd = lax.rem(tp, 2)
    row_at = [lax.rem(y + k, 4) * 8 for k in range(4)]
    col_at = [lax.rem(x + k, 4) * 2 for k in range(4)]
    core_at = [core, 1 - core]

    def static_away(d):
        k = d // 2
        return row_at[k % 4] + col_at[(k % 4 + k // 4) % 4] + core_at[d % 2]

    need = ((tp + 2) // 4) % 2

    def peer(k, sign, flip):
        step = lax.rem(k, 4)
        ny = lax.rem(y + sign * step + 4, 4)
        nx = lax.rem(x + sign * (step + lax.div(k, 4)) + 8, 4)
        return ny * 8 + nx * 2 + core_at[flip]

    def same(n, sign):
        corner = n - 7
        dy = jnp.where(n < 4, 0, jnp.where(n < 7, n - 3, 1 + lax.div(jnp.maximum(corner, 0), 3)))
        dx = jnp.where(n < 4, n, jnp.where(n < 7, 0, 1 + lax.rem(jnp.maximum(corner, 0), 3)))
        ny = lax.rem(y + sign * dy + 4, 4)
        nx = lax.rem(x + sign * dx + 4, 4)
        return ny * 8 + nx * 2 + core

    barrier = pltpu.get_barrier_semaphore()

    for d in range(1, 32):
        pl.semaphore_signal(barrier, inc=1, device_id={"seq": static_away(d)}, device_id_type=MESH)
    for d in range(1, 8):
        pl.semaphore_signal(barrier, inc=1, device_id={"tp": lax.rem(tp + d, 8)}, device_id_type=MESH)

    own_half = pltpu.make_async_copy(cache_ref, kv.at[:, core], kv_sem.at[0])
    own_half.start()
    loads = [
        pltpu.make_async_copy(src, dst, w_sem.at[i])
        for i, (src, dst) in enumerate(((wout_ref, wout), (wgu_ref, wgu), (wd_ref, wd)))
    ]
    for load in loads:
        load.start()

    asked = query_ref[...].astype(F32) * 0.125
    for h in range(8):
        qraw[:, h * 64 : h * 64 + 64] = asked[:, h * 64 : h * 64 + 64].T
    query = qraw[...].astype(BF)
    qown[...] = query
    qin[0] = query
    node = lax.broadcasted_iota(jnp.int32, (64, 16), 0)
    row = lax.broadcasted_iota(jnp.int32, (64, 16), 1)
    chosen = jnp.where((node == aidx_ref[...]) & (row < alen_ref[0]), 1.0, 0.0).astype(BF)
    picked = dot_tn(chosen, draft_ref[...]).astype(BF)
    tbuf[...] = picked
    tin[me] = picked

    pl.semaphore_wait(barrier, 38)
    swap = remote(cache_ref, kv.at[:, core], kv_sem.at[1], kv_sem.at[2], seq=chip * 2 + 1 - core)
    swap.start()

    def along(k):
        return row_at[0] + col_at[k] + core if k < 4 else row_at[k - 3] + col_at[0] + core

    def first_query(k):
        return remote(qown, qin.at[k], q_send.at[k], q_recv.at[k], seq=along(k))

    def relayed(axis, a, b):
        dy, dx = (b, a) if axis == 0 else (a, b)
        held, slot = (dx, 7 + 3 * (dy - 1) + dx - 1) if axis == 0 else (3 + dy, 7 + 3 * (dy - 1) + dx - 1)
        half = pl.ds(32 * axis, 32)
        return remote(
            qin.at[held, half], qin.at[slot, half], h_send.at[axis, slot], h_recv.at[axis, slot],
            seq=along(3 + b) if axis == 0 else along(b),
        )

    for k in range(1, 4):
        first_query(k).start()
        first_query(3 + k).start()
    for d in range(1, 32):
        remote(tbuf, tin.at[me], t_sem.at[0], t_sem.at[1], seq=static_away(d)).start()

    draft = draft_ref[...]
    up_id = lax.broadcasted_iota(jnp.int32, (64, 64), 0)
    node_id = lax.broadcasted_iota(jnp.int32, (64, 64), 1)
    reach = jnp.where((parents_ref[...] == up_id) | (up_id == node_id), 1.0, 0.0)
    for _ in range(6):
        half = reach.astype(BF)
        reach = jnp.minimum(dot(half, half), 1.0)
    allowed = jnp.concatenate([reach] * 8, axis=1) > 0.5
    tree = jnp.where(allowed, dot(draft, jnp.concatenate([query, jnp.zeros((64, 512), BF)], axis=0)), LOW)
    tree_max = jnp.max(tree, axis=0, keepdims=True)
    tree_weight = jnp.where(allowed, jnp.exp(tree - tree_max), 0.0)
    tree_sum = jnp.sum(tree_weight, axis=0, keepdims=True)
    tree_num = dot_tn(draft, tree_weight.astype(BF))[64:]

    expert_id = lax.broadcasted_iota(jnp.int32, (32, 64), 0)
    member = jnp.zeros((32, 64), F32)
    given = jnp.zeros((32, 64), F32)
    for k in range(4):
        hit = routes_ref[k : k + 1, :] == expert_id
        member = jnp.where(hit, 1.0, member)
        given = jnp.where(hit, weight_ref[k : k + 1, :], given)
    rank = dot(member.astype(BF), jnp.where(up_id < node_id, 1.0, 0.0).astype(BF))
    slot = lax.broadcasted_iota(jnp.int32, (16, 64), 0).astype(F32)
    for e in range(32):
        here = (slot == rank[e : e + 1, :]) & (member[e : e + 1, :] > 0.5)
        put[e * 16 : e * 16 + 16, :] = jnp.where(here, 1.0, 0.0).astype(BF)
        mix[e * 16 : e * 16 + 16, :] = jnp.where(here, given[e : e + 1, :], 0.0)
    for load in loads:
        load.wait()
    blank = jnp.zeros((360, 24), BF)
    for j in range(8):
        span, wide = slice(360 * j, 360 * j + 360), slice(384 * j, 384 * j + 384)
        wgp[0, :, wide] = jnp.concatenate([wgu[0, :, span], blank], axis=1)
        wgp[1, :, wide] = jnp.concatenate([wgu[1, :, span], blank], axis=1)
        wdp[:, wide] = jnp.concatenate([wd[:, span], blank], axis=1)
    zsend[...] = jnp.zeros((8, 64, 384), BF)
    hpad[...] = jnp.zeros((64, 384), F32)
    hpad[:, 0:360] = hidden_ref[...].astype(F32)
    gains[...] = jnp.zeros((8, 1, 384), F32)
    for j in range(8):
        gains[j, :, 0:360] = gain_ref[360 * j : 360 * j + 360].reshape(1, 360)

    own_half.wait()
    swap.wait()
    position = lax.broadcasted_iota(jnp.int32, (1024, 128), 0) + chip * 1024

    def attend(d):
        request = same(d, -1)

        @pl.when(d == 1)
        def _():
            for a in range(1, 4):
                for axis in range(2):
                    first_query(a + 3 * axis).wait_recv()
                    for b in range(1, 4):
                        relayed(axis, a, b).start()

        @pl.when(d > 6)
        def _():
            for axis in range(2):
                half = pl.ds(32 * axis, 32)
                remote(
                    qown.at[half], qin.at[d, half], h_send.at[axis, 0], h_recv.at[axis, d], seq=request
                ).wait_recv()

        group = group_ref[request]
        length = len_ref[group]
        cached = kv[group].reshape(1024, 128)
        bias = jnp.where(position < length, 0.0, LOW)
        bias = jnp.concatenate([bias, bias], axis=1)
        halves = (slice(0, 256), slice(256, 512))
        scores = [
            dot(cached, jnp.concatenate([qin[d, :, cols], jnp.zeros((64, 256), BF)], axis=0)) + bias
            for cols in halves
        ]
        for cols, score in zip(halves, scores):
            top = jnp.maximum(jnp.max(score, axis=0, keepdims=True), FLOOR)
            weight = jnp.exp(score - top)
            total = jnp.sum(weight, axis=0, keepdims=True)
            value = dot_tn(cached, weight.astype(BF))[64:]
            obuf[d, :, cols] = (value / jnp.maximum(total, 1.0)).astype(BF)
            sbuf[d, 0:1, cols] = top
            sbuf[d, 1:2, cols] = total

        @pl.when(d > 0)
        def _():
            remote(obuf.at[d], oin.at[d], o_send.at[d], o_recv.at[d], seq=request).start()
            remote(sbuf.at[d], sin.at[d], s_send.at[d], s_recv.at[d], seq=request).start()

    loop(0, 16, attend)
    oin[0] = obuf[0]
    sin[0] = sbuf[0]

    lane = lax.broadcasted_iota(jnp.int32, (1, 512), 1)
    sink = jnp.zeros((1, 512), F32)
    for h in range(8):
        sink = jnp.where(lane // 64 == h, sink_ref[h], sink)

    def land(d):
        other = same(d, 1)
        remote(obuf.at[d], oin.at[d], o_send.at[d], o_recv.at[d], seq=other).wait()
        remote(sbuf.at[d], sin.at[d], s_send.at[d], s_recv.at[d], seq=other).wait()

    ceiling = jnp.maximum(tree_max, sink)
    tree_scale = jnp.exp(tree_max - ceiling)
    below = tree_scale * tree_sum + jnp.exp(sink - ceiling)
    above = tree_scale * tree_num
    for first in range(0, 16, 4):
        loop(max(first, 1), first + 4, land)
        before = ceiling
        for d in range(first, first + 4):
            ceiling = jnp.maximum(ceiling, sin[d, 0:1])
        fade = jnp.exp(before - ceiling)
        below = below * fade
        above = above * fade
        for d in range(first, first + 4):
            scale = sin[d, 1:2] * jnp.exp(sin[d, 0:1] - ceiling)
            below = below + scale
            above = above + scale * oin[d].astype(F32)
    for a in range(1, 4):
        for axis in range(2):
            first_query(a + 3 * axis).wait_send()
            for b in range(1, 4):
                relayed(axis, a, b).wait_send()
    merged = above / below
    for h in range(8):
        att[:, h * 64 : h * 64 + 64] = merged[:, h * 64 : h * 64 + 64].T
    attended = att[...].astype(BF)
    for j in range(8):
        zsend[j, :, 0:360] = dot_nt(attended, wout[360 * j : 360 * j + 360, :]).astype(BF)

    def send_piece(d):
        to = (tp + d) % 8
        remote(zsend.at[to], zrecv.at[d], z_send.at[d], z_recv.at[d], tp=to).start()

    loop(1, 8, send_piece)
    def drain(ref, sem):
        pltpu.make_async_copy(ref.at[pl.ds(0, 31)], ref.at[pl.ds(0, 31)], sem).wait()

    drain(tin, t_sem.at[0])
    drain(tin, t_sem.at[1])
    kept = jnp.zeros((16, 128), F32)
    for r in range(32):
        kept = kept + jnp.where(slot_ref[r] == me, tin[r].astype(F32), 0.0)
    tail_ref[...] = kept.astype(BF)
    total = hpad[...] + zsend[tp].astype(F32)
    for d in range(1, 8):
        remote(zsend.at[d], zrecv.at[d], z_send.at[d], z_recv.at[d], tp=(tp + d) % 8).wait()
        total = total + zrecv[d].astype(F32)
    stream = total.astype(BF)
    piece[...] = stream
    stream_f = stream.astype(F32)

    for k in range(4):
        to = 2 * k + need

        @pl.when(to != tp)
        def _(k=k, to=to):
            remote(piece, gall.at[tp % 4], g_send.at[k], g_recv.at[tp % 4], tp=to).start()

        @pl.when(to == tp)
        def _():
            gall[tp % 4] = piece[...]

    squares = jnp.sum(stream_f * stream_f, axis=1, keepdims=True)
    square = jnp.broadcast_to(squares, (64, 128))
    spread_rows = jnp.concatenate([square, square], axis=0).T[0:8]
    ssend[...] = spread_rows

    def send_norm(d):
        remote(ssend, srecv.at[d], n_send.at[d], n_recv.at[d], tp=(tp + d) % 8).start()

    loop(1, 8, send_norm)
    summed = spread_rows
    for d in range(1, 8):
        remote(ssend, srecv.at[d], n_send.at[d], n_recv.at[d], tp=(tp + d) % 8).wait()
        summed = summed + srecv[d]
    column = jnp.concatenate([summed] * 16, axis=0).T[0:64, 0:1]
    inverse = lax.rsqrt(column * (1.0 / 2880.0) + 1e-05)

    for k in range(4):
        source = k + 4 * ((k // 2 + odd) % 2)

        @pl.when(source != tp)
        def _(k=k, source=source):
            remote(piece, gall.at[k], g_send.at[k], g_recv.at[k], tp=source).wait_recv()

    mine = (odd, 3 - odd)
    for h in range(2):
        for i in range(2):
            j = 2 * mine[h] + i
            normed = gall[j % 4].astype(F32) * inverse * gains[j]
            nq[h, :, 384 * i : 384 * i + 384] = normed.astype(BF)

    for h in range(2):
        @pl.loop(0, 4)
        def _(b, h=h):
            rows = put[pl.ds(pl.multiple_of(b * 128, 128), 128), :]
            sent[h, pl.ds(b * 8, 8)] = dot(rows, nq[h]).astype(BF).reshape(8, 16, 768)

    def dispatch(g, first=0):
        for i in range(first, SIZE):
            to = peer(SIZE // 2 * g + i // 2, 1, i % 2)
            d = SIZE * g + i
            for h in range(2):
                remote(
                    sent.at[h, to], arrived.at[mine[h], d], d_send.at[h, g], d_recv.at[h, d], seq=to
                ).start()

    def dispatched(g, count):
        for h in range(2):
            block = sent.at[h, pl.ds(0, count)]
            pltpu.make_async_copy(block, block, d_send.at[h, g]).wait()

    dispatch(0, 1)
    for g in range(1, AHEAD):
        dispatch(g)
    for h in range(2):
        arrived[mine[h], 0] = sent[h, me]

    partner = (tp + 1 - 2 * odd, lax.rem(tp + 7 + 2 * odd, 8))
    other = (1 - odd, 2 + odd)

    def forward(g):
        for i in range(SIZE):
            d = SIZE * g + i
            for h in range(2):
                @pl.when(d > 0)
                def _(h=h, d=d):
                    remote(
                        sent.at[h, 0], arrived.at[mine[h], d], d_send.at[h, 0], d_recv.at[h, d],
                        seq=static_away(1),
                    ).wait_recv()

                block = arrived.at[mine[h], d]
                remote(block, block, f_send.at[h], f_recv.at[h, g], tp=partner[h]).start()

    def feed(g):
        for h in range(2):
            block = arrived.at[other[h], pl.ds(g * SIZE, SIZE)]
            pltpu.make_async_copy(block, block, f_recv.at[h, g]).wait()
        gate = jnp.zeros((16 * SIZE, 360), F32)
        up = jnp.zeros((16 * SIZE, 360), F32)
        for q in range(4):
            rows = arrived[q, pl.ds(g * SIZE, SIZE)].reshape(16 * SIZE, 768)
            cols = slice(768 * q, 768 * q + 768)
            gate = gate + dot_nt(rows, wgp[0, :, cols])
            up = up + dot_nt(rows, wgp[1, :, cols])
        act = (gate * jax.nn.sigmoid(1.702 * gate) * (up + 1.0)).astype(BF)
        for h in range(2):
            far = dot(act, wdp[:, pl.ds(pl.multiple_of(768 * other[h], 128), 768)])
            zout[h, g] = far.astype(BF).reshape(SIZE, 16, 768)
            remote(zout.at[h, g], zin.at[h, g], p_send.at[h, g], p_recv.at[h, g], tp=partner[h]).start()
        for h in range(2):
            keep[h, g] = dot(act, wdp[:, pl.ds(pl.multiple_of(768 * mine[h], 128), 768)])

    def give(g):
        for h in range(2):
            remote(zout.at[h, g], zin.at[h, g], p_send.at[h, g], p_recv.at[h, g], tp=partner[h]).wait()
            both = keep[h, g] + zin[h, g].reshape(16 * SIZE, 768).astype(F32)
            back[h, pl.ds(g * SIZE, SIZE)] = both.astype(BF).reshape(SIZE, 16, 768)

        for i in range(SIZE):
            to = peer(SIZE // 2 * g + i // 2, -1, i % 2)
            d = SIZE * g + i
            for h in range(2):
                @pl.when(d > 0)
                def _(h=h, d=d, to=to):
                    remote(back.at[h, d], got.at[h, me], b_send.at[h], b_recv.at[h], seq=to).start()

    def stage(i):
        @pl.when(i == 0)
        def _():
            dispatched(0, SIZE - 1)

        @pl.when((i > 0) & (i < GROUPS))
        def _():
            dispatched(i, SIZE)

        @pl.when(i < GROUPS - AHEAD)
        def _():
            dispatch(i + AHEAD)

        @pl.when(i < GROUPS)
        def _():
            forward(i)

        @pl.when((i >= FEED_LAG) & (i < GROUPS + FEED_LAG))
        def _():
            feed(i - FEED_LAG)

        @pl.when(i >= GIVE_LAG)
        def _():
            give(i - GIVE_LAG)

    loop(0, GROUPS + GIVE_LAG, stage)
    for h in range(2):
        got[h, me] = back[h, 0]

    weight = mix[...].T
    high = weight.astype(BF)
    low = (weight - high.astype(F32)).astype(BF)
    mixing = jnp.concatenate([high, low], axis=0)

    for h in range(2):
        drain(got.at[h], b_recv.at[h])
        both = dot(mixing, got[h].reshape(512, 768))
        both = both[0:64] + both[64:128]
        for i in range(2):
            k = 2 * h + i
            to = 2 * mine[h] + i
            fsend[k] = both[:, 384 * i : 384 * i + 384].astype(BF)

            @pl.when(to != tp)
            def _(k=k, to=to):
                remote(fsend.at[k], frecv.at[tp // 2], e_send.at[k], e_recv.at[tp // 2], tp=to).start()

            @pl.when(to == tp)
            def _(k=k):
                frecv[tp // 2] = fsend[k]

    total = piece[...].astype(F32)
    for k in range(4):
        source = 2 * k + need

        @pl.when(source != tp)
        def _(k=k, source=source):
            remote(fsend.at[k], frecv.at[k], e_send.at[k], e_recv.at[k], tp=source).wait_recv()

        total = total + frecv[k].astype(F32)
    out_ref[...] = total[:, 0:360].astype(BF)


    for k in range(4):
        @pl.when(2 * k + need != tp)
        def _(k=k):
            remote(piece, gall.at[k], g_send.at[k], g_recv.at[k], tp=2 * k + need).wait_send()

        to = 2 * mine[k // 2] + k % 2

        @pl.when(to != tp)
        def _(k=k, to=to):
            remote(fsend.at[k], frecv.at[k], e_send.at[k], e_recv.at[k], tp=to).wait_send()

    for h in range(2):
        drain(back.at[h], b_send.at[h])
        pltpu.make_async_copy(sent.at[h], sent.at[h], f_send.at[h]).wait()


def run_layer(*operands):
    smem = pl.BlockSpec(memory_space=pltpu.SMEM)
    vmem = pl.BlockSpec(memory_space=pltpu.VMEM)
    hbm = pl.BlockSpec(memory_space=pl.ANY)
    dma = pltpu.SemaphoreType.DMA
    return pl.pallas_call(
        layer_kernel,
        out_shape=(jax.ShapeDtypeStruct((64, 360), BF), jax.ShapeDtypeStruct((16, 128), BF)),
        in_specs=[smem] * 5 + [vmem, vmem, hbm, vmem, vmem, hbm, vmem, vmem, vmem, vmem, hbm, hbm],
        out_specs=(vmem, vmem),
        scratch_shapes=[
            pltpu.VMEM((8, 2, 512, 128), BF),
            pltpu.VMEM((64, 512), F32),
            pltpu.VMEM((64, 512), BF),
            pltpu.VMEM((16, 64, 512), BF),
            pltpu.VMEM((16, 64, 512), BF),
            pltpu.VMEM((16, 2, 512), F32),
            pltpu.VMEM((16, 64, 512), BF),
            pltpu.VMEM((16, 2, 512), F32),
            pltpu.VMEM((16, 128), BF),
            pltpu.VMEM((32, 16, 128), BF),
            pltpu.VMEM((64, 512), F32),
            pltpu.VMEM((2880, 512), BF),
            pltpu.VMEM((64, 384), F32),
            pltpu.VMEM((8, 64, 384), BF),
            pltpu.VMEM((8, 64, 384), BF),
            pltpu.VMEM((64, 384), BF),
            pltpu.VMEM((4, 64, 384), BF),
            pltpu.VMEM((8, 128), F32),
            pltpu.VMEM((8, 8, 128), F32),
            pltpu.VMEM((2, 64, 768), BF),
            pltpu.VMEM((2, 360, 2880), BF),
            pltpu.VMEM((2, 360, 3072), BF),
            pltpu.VMEM((360, 2880), BF),
            pltpu.VMEM((360, 3072), BF),
            pltpu.VMEM((512, 64), BF),
            pltpu.VMEM((512, 64), F32),
            pltpu.VMEM((2, 32, 16, 768), BF),
            pltpu.VMEM((4, 32, 16, 768), BF),
            pltpu.VMEM((2, GROUPS, SIZE, 16, 768), BF),
            pltpu.VMEM((2, GROUPS, SIZE, 16, 768), BF),
            pltpu.VMEM((2, GROUPS, 16 * SIZE, 768), F32),
            pltpu.VMEM((2, 32, 16, 768), BF),
            pltpu.VMEM((2, 32, 16, 768), BF),
            pltpu.VMEM((8, 1, 384), F32),
            pltpu.VMEM((4, 64, 384), BF),
            pltpu.VMEM((4, 64, 384), BF),
            dma((3,)), dma((7,)), dma((7,)), dma((2, 16)), dma((2, 16)), dma((16,)), dma((16,)), dma((16,)), dma((16,)),
            dma((2,)), dma((3,)),
            dma((8,)), dma((8,)), dma((4,)), dma((4,)), dma((8,)), dma((8,)),
            dma((2, GROUPS)), dma((2, 32)), dma((2,)), dma((2, GROUPS)), dma((2, GROUPS)), dma((2, GROUPS)),
            dma((2,)), dma((2,)), dma((4,)), dma((4,)),
        ],
        compiler_params=pltpu.CompilerParams(
            collective_id=0, has_side_effects=True, vmem_limit_bytes=62 * 1024 * 1024
        ),
        name="layer",
    )(*operands)


def hand_over_kernel(out_ref, tail_ref, out_to, tail_to):
    out_to[...] = out_ref[...]
    tail_to[...] = tail_ref[...]


def hand_over(out, tail):
    vmem = pl.BlockSpec(memory_space=pltpu.VMEM)
    return pl.pallas_call(
        hand_over_kernel,
        out_shape=(jax.ShapeDtypeStruct(out.shape, BF), jax.ShapeDtypeStruct(tail.shape, BF)),
        in_specs=[vmem, vmem],
        out_specs=(vmem, vmem),
        name="hand_over",
    )(out, tail)


def shards(
    queries, draft_kv, cache_kv, cache_len, group_of, parents, sink_logit, w_out, hidden_in,
    norm_gain, routes, route_weight, w_gate_up, w_down, accepted_idx, accepted_len, tail_slot,
):
    out, tail = run_layer(
        group_of, cache_len, sink_logit, tail_slot, accepted_len,
        queries.reshape(64, 512), draft_kv.reshape(64, 128), cache_kv.reshape(8, 512, 128), parents,
        accepted_idx, w_out.T, hidden_in, norm_gain, routes.T, route_weight.T,
        w_gate_up.reshape(2, 2880, 360).transpose(0, 2, 1), w_down.reshape(360, 2880),
    )
    out, tail = hand_over(out, tail)
    return (out, tail.reshape(1, 16, 1, 128))


def solution(mesh):
    in_specs = (
        P("seq", None, "tp"),
        P("seq", None, "tp", None),
        P(None, "seq", "tp", None),
        P(),
        P(),
        P("seq", None),
        P("tp"),
        P("tp", None),
        P("seq", "tp"),
        P(),
        P("seq", None),
        P("seq", None),
        P("seq", None, None, "tp"),
        P("seq", "tp", None),
        P("seq", None),
        P("seq"),
        P(),
    )
    out_specs = (P("seq", "tp"), P("seq", None, "tp", None))
    return jax.shard_map(shards, mesh=mesh, in_specs=in_specs, out_specs=out_specs, check_vma=False)
```
